512 devices in a mesh: root: 4 (over z_hi, core), col: 128 (over z_lo, y, x).
Axes of the slice: x: 4, y: 4, z: 16 (z_hi: 2, z_lo: 8; z = z_hi * 8 + z_lo), core: 2. Of those that a mesh axis runs over, the one named last changes fastest.
Arguments:
- coeffs: float32 [4, 3072, 3072], P('root', 'col'), may hold values from -6 to 6
- diagonal: float32 [3072, 3072], P('col'), may hold values from -1 to 1
- shift: float32 [4], P('root'), may hold values from -1 to 1
- rotation: float32 [4, 4], replicated, may hold values from -1 to 1, as said below
- string_blocks: bfloat16 [30720, 128], P('col'), may hold values from -0.15625 to 0.15625
- block_cols: int32 [24, 10], replicated, may hold values from 0 to 23, all different within a row
Outputs:
- filtered: float32 [4, 3072, 3072], P('root', 'col')
The draws below stay inside these ranges and needn't reach their ends.
Inputs may be any that keep to these rules, and one draw needn't show every extreme that they name: `block_cols`: each row names 10 different block columns, and every block column is named by some row. rotation is an orthogonal matrix.
All inputs are finite; a program needn't handle non-finite values.
Results may differ from the reference program's by a relative error of at most 0.0003.
Values may be sent and summed in bfloat16 or wider, within the bound.
A program may use at most 64 MiB of HBM per device.

```python
import jax
import jax.numpy as jnp
from jax import lax

STRINGS = 3072
BLK = 128
FILL = 10
NBLK = 24
ROOTS = 4


def draw_rotation(key, part):
    raw = jax.random.normal(jax.random.fold_in(key, 17), (ROOTS, ROOTS), jnp.float32)
    vectors = []
    for index in range(ROOTS):
        current = raw[index]
        for earlier in vectors:
            current = current - jnp.dot(earlier, current) * earlier
        current = current / jnp.sqrt(jnp.sum(current * current))
        vectors.append(current)
    return jnp.stack(vectors, axis=0)


def steps_of(key, dims, shards, smallest, high):
    def one(dim, blocks):
        steps = jax.random.uniform(jax.random.fold_in(jax.random.fold_in(key, 6), dim), (blocks,), jnp.float32, smallest / len(shards), high / len(shards))
        return jnp.repeat(jnp.exp(steps), dims[dim] // blocks).reshape((-1,) + (1,) * (len(dims) - dim - 1))

    loudness = one(*shards[0])
    for cut in shards[1:]:
        loudness = loudness * one(*cut)
    return loudness


def picks_of(stream_key, rows, number_of, top, lift):
    order = jax.random.permutation(jax.random.fold_in(stream_key, 1), number_of)
    boost = order
    for power in range(3):
        boost = boost * boost // number_of
    boost = boost * lift // number_of
    lots = jax.random.randint(jax.random.fold_in(stream_key, 2), (rows, number_of), 0, 4096) + boost
    sure = jax.random.permutation(jax.random.fold_in(stream_key, 3), rows)[jnp.arange(number_of) % rows]
    lots = jnp.where(jnp.arange(rows)[:, None] == sure[None, :], 1 << 14, lots)
    priority = lots * number_of + jnp.arange(number_of)
    return lax.top_k(priority.astype(jnp.int32), top)[1].astype(jnp.int32)


def gaussian(key, extent, spread, bound, split=(), dtype=jnp.bfloat16):
    gain = steps_of(key, extent, split, -0.22, 0.18) if split else 1.0
    entries = jax.random.normal(key, extent, jnp.float32) * spread * gain
    return jnp.minimum(jnp.maximum(entries, -bound), bound).astype(dtype)


def setup_inputs(seed: int = 0) -> dict:
    arg_keys = jax.random.split(jax.random.key(seed), 7)
    coeffs = gaussian(arg_keys[0], (ROOTS, STRINGS, STRINGS), 1.0, 6.0, ((0, 4), (1, 128)), jnp.float32)
    diagonal = jnp.clip(jax.random.uniform(arg_keys[1], (STRINGS, STRINGS), jnp.float32, -1.0, 1.0) * steps_of(arg_keys[1], (STRINGS, STRINGS), ((0, 128),), -0.4, 0.0), -1.0, 1.0)
    shift = jnp.clip(jax.random.uniform(arg_keys[2], (ROOTS,), jnp.float32, -1.0, 1.0) * steps_of(arg_keys[2], (ROOTS,), ((0, 4),), -0.4, 0.0), -1.0, 1.0)
    rotation = draw_rotation(jax.random.fold_in(arg_keys[6], 71), 0)
    string_blocks = gaussian(arg_keys[4], (NBLK * FILL * BLK, BLK), (FILL * BLK) ** -0.5, 0.15625, ((0, 128),))
    block_cols = picks_of(arg_keys[5], NBLK, NBLK, FILL, 0)
    return {"coeffs": coeffs, "diagonal": diagonal, "shift": shift, "rotation": rotation, "string_blocks": string_blocks, "block_cols": block_cols}


def apply_blocks(matrix, string_blocks, block_cols):
    height, breadth = matrix.shape
    nblocks, filled = block_cols.shape
    blocksize = breadth // nblocks
    grouped = matrix.reshape(height, nblocks, blocksize)
    picked = jnp.take(grouped, block_cols, axis=1).astype(jnp.float32)
    tiles = string_blocks.reshape(nblocks, filled, blocksize, blocksize).astype(jnp.float32)
    result = jnp.einsum("rifk,ifjk->rij", picked, tiles, precision=lax.Precision.HIGHEST)
    return result.reshape(height, breadth)


def apply_rows(matrix, string_blocks, block_cols):
    breadth = matrix.shape[1]
    stacked = matrix.reshape(-1, 256, breadth)
    result = lax.map(lambda piece: apply_blocks(piece, string_blocks, block_cols), stacked)
    return result.reshape(-1, breadth)


def sigma(vector, diagonal, string_blocks, block_cols):
    alpha_part = apply_rows(vector, string_blocks, block_cols)
    beta_part = apply_rows(vector.T, string_blocks, block_cols).T
    return alpha_part + beta_part + diagonal * vector


def reference(coeffs, diagonal, shift, rotation, string_blocks, block_cols):
    seconds = []
    for index in range(ROOTS):
        start = coeffs[index]
        energy = shift[index]
        first = 0.5 * (sigma(start, diagonal, string_blocks, block_cols) - energy * start)
        second = (sigma(first, diagonal, string_blocks, block_cols) - energy * first) - start
        seconds.append(second)
    stacked = jnp.stack(seconds, axis=0)
    return jnp.einsum("rs,sba->rba", rotation, stacked, precision=lax.Precision.HIGHEST)
```

```python
import functools

import jax
import jax.numpy as jnp
from jax import lax
from jax.experimental import pallas as pl
from jax.experimental.pallas import tpu as pltpu
from jax.sharding import Mesh
from jax.sharding import PartitionSpec as P

ROOT = ("zh", "core")
COL = ("zl", "y", "x")
CUT = 128


def place(**moved):
    z = lax.axis_index("zh") * 8 + lax.axis_index("zl")
    z = lax.rem(z + moved.get("z", 0) + 16, 16)
    return {
        "zh": z // 8,
        "core": lax.rem(lax.axis_index("core") + moved.get("core", 0), 2),
        "zl": lax.rem(z, 8),
        "y": lax.rem(lax.axis_index("y") + moved.get("y", 0) + 4, 4),
        "x": lax.rem(lax.axis_index("x") + moved.get("x", 0) + 4, 4),
    }


def gather_kernel(mine_ref, full_ref, send_sems, recv_sems, local_sem):
    core = lax.axis_index("core")
    here = place()
    barrier = pltpu.get_barrier_semaphore()
    peers = [{"z": d} for d in (1, 2, 3, 4, -1, -2, -3, -4)]
    peers += [{"y": 1}, {"y": -1}, {"x": 1}, {"x": -1}, {"core": 1}]
    for step in peers:
        pl.semaphore_signal(barrier, inc=1, device_id=place(**step), device_id_type=pl.DeviceIdType.MESH)

    pl.semaphore_wait(barrier, len(peers))

    def spread(color):
        rows = pl.ds(0, CUT) if color == 0 else pl.ds(CUT, 240 - CUT)
        other_rows = pl.ds(CUT, 240 - CUT) if color == 0 else pl.ds(0, CUT)
        first, second = ("y", "x") if color == 0 else ("x", "y")
        pending = []
        counter = [0]

        def part(zl, a, b, rows_=None, swap=False):
            rows_ = rows if rows_ is None else rows_
            a_first = (first == "y") != swap
            y, x = (a, b) if a_first else (b, a)
            return full_ref.at[zl, y, x, rows_]

        def at(step):
            return lax.rem(here[first] + step + 4, 4)

        def bt(step):
            return lax.rem(here[second] + step + 4, 4)

        def exchange(mine, theirs, to):
            k = counter[0]
            counter[0] += 1
            copy = pltpu.make_async_remote_copy(
                src_ref=mine, dst_ref=mine, send_sem=send_sems.at[k], recv_sem=recv_sems.at[k],
                device_id=place(**to), device_id_type=pl.DeviceIdType.MESH)
            copy.start()
            pending.append(copy)
            landing = pltpu.make_async_remote_copy(
                src_ref=theirs, dst_ref=theirs, send_sem=send_sems.at[k], recv_sem=recv_sems.at[k],
                device_id=place(**to), device_id_type=pl.DeviceIdType.MESH)
            return landing.wait_recv

        every = pl.ds(0, 8)
        halves = (pl.ds(0, 4), pl.ds(4, 4))
        own = pltpu.make_async_copy(mine_ref.at[rows], part(here["zl"], here[first], here[second]), local_sem)
        own.start()
        own.wait()

        waits = []
        for d in (1, -1, 2, -2, 3, -3, 4):
            zl_from = lax.rem(here["zl"] - d + 8, 8)
            waits.append(exchange(part(here["zl"], here[first], here[second]),
                                  part(zl_from, here[first], here[second]), {"z": d}))
        for wait in waits:
            wait()

        sibling = []

        def to_sibling(zl, a, b):
            k = counter[0]
            counter[0] += 1
            copy = pltpu.make_async_remote_copy(
                src_ref=part(zl, a, b), dst_ref=part(zl, a, b), send_sem=send_sems.at[k], recv_sem=recv_sems.at[k],
                device_id=place(core=1), device_id_type=pl.DeviceIdType.MESH)
            copy.start()
            pending.append(copy)

        def from_sibling(zl, a, b):
            k = counter[0]
            counter[0] += 1
            ref = part(zl, a, b, other_rows, True)
            sibling.append(pltpu.make_async_remote_copy(
                src_ref=ref, dst_ref=ref, send_sem=send_sems.at[k], recv_sem=recv_sems.at[k],
                device_id=place(core=1), device_id_type=pl.DeviceIdType.MESH))

        a0, b0 = at(0), bt(0)
        first_waits = {}
        first_waits[1] = exchange(part(every, a0, b0), part(every, at(-1), b0), {first: 1})
        first_waits[-1] = exchange(part(every, a0, b0), part(every, at(1), b0), {first: -1})
        second_waits = []

        def along_second(zl, step, down, up):
            wait_up = exchange(part(zl, at(step), b0), part(zl, at(step), bt(-1)), {second: 1})
            wait_down = exchange(part(zl, at(step), b0), part(zl, at(step), bt(1)), {second: -1})
            second_waits.append((step, zl, down, up, wait_up, wait_down))

        along_second(every, 0, *halves)
        to_log = [(every, 0, 0)]
        to_sibling(every, a0, b0)
        first_waits[1]()
        far_low = exchange(part(halves[0], at(-1), b0), part(halves[0], at(-2), b0), {first: 1})
        along_second(every, -1, *halves)
        to_sibling(every, at(-1), b0)
        first_waits[-1]()
        far_high = exchange(part(halves[1], at(1), b0), part(halves[1], at(2), b0), {first: -1})
        along_second(every, 1, *halves)
        to_sibling(every, at(1), b0)
        quarters = (pl.ds(0, 2), pl.ds(2, 2), pl.ds(4, 2), pl.ds(6, 2))
        far_low()
        along_second(halves[0], 2, quarters[0], quarters[1])
        to_sibling(halves[0], at(2), b0)
        far_high()
        along_second(halves[1], 2, quarters[2], quarters[3])
        to_sibling(halves[1], at(2), b0)

        last = []
        for step, zl, low, high, wait_up, wait_down in second_waits:
            wait_up()
            last.append((step, low, exchange(part(low, at(step), bt(-1)), part(low, at(step), bt(-2)), {second: 1})))
            to_sibling(zl, at(step), bt(-1))
            wait_down()
            last.append((step, high, exchange(part(high, at(step), bt(1)), part(high, at(step), bt(2)), {second: -1})))
            to_sibling(zl, at(step), bt(1))
        for step, zl, wait in last:
            wait()
            to_sibling(zl, at(step), bt(2))

        for copy in pending:
            copy.wait_send()
        sends = counter[0]
        return sends

    def sibling_waits(color):
        rows = pl.ds(CUT, 240 - CUT) if color == 0 else pl.ds(0, CUT)
        first, second = ("x", "y") if color == 0 else ("y", "x")

        def at(step):
            return lax.rem(here[first] + step + 4, 4)

        def bt(step):
            return lax.rem(here[second] + step + 4, 4)

        def wait(k, zl, a, b):
            y, x = (a, b) if first == "y" else (b, a)
            ref = full_ref.at[zl, y, x, rows]
            pltpu.make_async_remote_copy(
                src_ref=ref, dst_ref=ref, send_sem=send_sems.at[k], recv_sem=recv_sems.at[k],
                device_id=place(core=1), device_id_type=pl.DeviceIdType.MESH).wait_recv()

        return wait, at, bt

    for color in (0, 1):
        @pl.when(core == color)
        def _():
            spread(color)
            wait, at, bt = sibling_waits(color)
            e = pl.ds(0, 8)
            h = (pl.ds(0, 4), pl.ds(4, 4))
            q = (pl.ds(0, 2), pl.ds(2, 2), pl.ds(4, 2), pl.ds(6, 2))
            k = 7
            k += 2
            k += 2
            wait(k, e, at(0), bt(0)); k += 1
            k += 3
            wait(k, e, at(-1), bt(0)); k += 1
            k += 3
            wait(k, e, at(1), bt(0)); k += 1
            k += 2
            wait(k, h[0], at(2), bt(0)); k += 1
            k += 2
            wait(k, h[1], at(2), bt(0)); k += 1
            sets = [(0, e, h[0], h[1]), (-1, e, h[0], h[1]), (1, e, h[0], h[1]),
                    (2, h[0], q[0], q[1]), (2, h[1], q[2], q[3])]
            for step, zl, low, high in sets:
                k += 1
                wait(k, zl, at(step), bt(-1)); k += 1
                k += 1
                wait(k, zl, at(step), bt(1)); k += 1
            for step, zl, low, high in sets:
                wait(k, low, at(step), bt(2)); k += 1
                wait(k, high, at(step), bt(2)); k += 1


MESSAGES = 64


def gather_operator(string_blocks):
    full = pl.pallas_call(
        gather_kernel,
        out_shape=jax.ShapeDtypeStruct((8, 4, 4, 240, 128), jnp.bfloat16),
        in_specs=[pl.BlockSpec(memory_space=pl.ANY)],
        out_specs=pl.BlockSpec(memory_space=pl.ANY),
        scratch_shapes=[
            pltpu.SemaphoreType.DMA((MESSAGES,)),
            pltpu.SemaphoreType.DMA((MESSAGES,)),
            pltpu.SemaphoreType.DMA,
        ],
        compiler_params=pltpu.CompilerParams(collective_id=0, has_side_effects=True),
        name="gather_operator",
    )(string_blocks)
    return full.reshape(30720, 128)


def apply_blocks(matrix, operator_blocks, block_cols):
    height, breadth = matrix.shape
    nblocks, filled = block_cols.shape
    blocksize = breadth // nblocks
    grouped = matrix.reshape(height, nblocks, blocksize)
    picked = jnp.take(grouped, block_cols, axis=1)
    tiles = operator_blocks.reshape(nblocks, filled, blocksize, blocksize).astype(jnp.float32)
    result = jnp.einsum("rifk,ifjk->rij", picked, tiles, precision=lax.Precision.HIGHEST)
    return result.reshape(height, breadth)


def layout_pieces(stacked):
    count, height, breadth = stacked.shape
    groups = breadth // height
    return (
        stacked.reshape(count, height, groups, height)
        .transpose(0, 2, 1, 3)
        .reshape(count, groups, height * height)
    )


def layout_whole(moved, height):
    count = moved.shape[0]
    groups = moved.shape[1]
    return (
        moved.reshape(count, groups, height, height)
        .transpose(0, 3, 1, 2)
        .reshape(count, height, groups * height)
    )


def swap_layout(stacked):
    moved = lax.all_to_all(layout_pieces(stacked), COL, split_axis=1, concat_axis=1, tiled=True)
    return layout_whole(moved, stacked.shape[1])


def shards(coeffs, diagonal, shift, rotation, string_blocks, block_cols):
    start = coeffs[0]
    energy = shift[0]
    operator_blocks = gather_operator(string_blocks)

    def apply_local(matrix):
        return apply_blocks(matrix, operator_blocks, block_cols)

    def sigma_local(vector):
        turned = swap_layout(vector[None])[0]
        beta_turned = apply_local(turned)
        beta_part = swap_layout(beta_turned[None])[0]
        return apply_local(vector) + beta_part + diagonal * vector

    first = 0.5 * (sigma_local(start) - energy * start)
    second = sigma_local(first) - energy * first - start
    all_roots = lax.all_gather(second[None], ROOT, axis=0, tiled=True)
    root = lax.axis_index("zh") * 2 + lax.axis_index("core")
    weights = lax.dynamic_index_in_dim(rotation, root, 0, keepdims=False)
    result = jnp.einsum("s,sba->ba", weights, all_roots, precision=lax.Precision.HIGHEST)
    return result[None]


def solution(mesh):
    split = Mesh(mesh.devices.reshape(2, 2, 8, 4, 4), ROOT + COL)
    return jax.shard_map(
        shards,
        mesh=split,
        in_specs=(P(ROOT, COL, None), P(COL, None), P(ROOT), P(), P(COL, None), P()),
        out_specs=P(ROOT, COL, None),
        check_vma=False,
    )
```

```python
import jax
import jax.numpy as jnp
from jax import lax
from jax.experimental import pallas as pl
from jax.experimental.pallas import tpu as pltpu
from jax.sharding import Mesh
from jax.sharding import PartitionSpec as P

ROOT = ("zh", "core")
COL = ("zl", "y", "x")
CUT = 128
F32, BF16 = jnp.float32, jnp.bfloat16
ONTO = pl.DeviceIdType.MESH

E, H, Q = (0, 8), ((0, 4), (4, 4)), ((0, 2), (2, 2), (4, 2), (6, 2))
Z_STEPS = (1, -1, 2, -2, 3, -3, 4)


def spread_plan():
    plan = [("z", ("z", d), None) for d in Z_STEPS]

    def both(zs, a):
        plan.append(((zs, a, 0), ("second", 1), (zs, a, -1)))
        plan.append(((zs, a, 0), ("second", -1), (zs, a, 1)))

    def sibling(zs, a, b):
        plan.append(((zs, a, b), ("core", 1), "sibling"))

    plan.append(((E, 0, 0), ("first", 1), (E, -1, 0)))
    plan.append(((E, 0, 0), ("first", -1), (E, 1, 0)))
    both(E, 0)
    sibling(E, 0, 0)
    marks = {"start": (7, 12)}
    steps = []
    n = len(plan)
    plan.append(((H[0], -1, 0), ("first", 1), (H[0], -2, 0)))
    both(E, -1)
    sibling(E, -1, 0)
    steps.append((7, (n, len(plan))))
    far_low = n
    n = len(plan)
    plan.append(((H[1], 1, 0), ("first", -1), (H[1], 2, 0)))
    both(E, 1)
    sibling(E, 1, 0)
    steps.append((8, (n, len(plan))))
    far_high = n
    n = len(plan)
    both(H[0], 2)
    sibling(H[0], 2, 0)
    steps.append((far_low, (n, len(plan))))
    n = len(plan)
    both(H[1], 2)
    sibling(H[1], 2, 0)
    steps.append((far_high, (n, len(plan))))
    sets = [(0, E, H[0], H[1], 9), (-1, E, H[0], H[1], 13), (1, E, H[0], H[1], 17),
            (2, H[0], Q[0], Q[1], 20), (2, H[1], Q[2], Q[3], 23)]
    last = []
    for a, zs, low, high, number in sets:
        n = len(plan)
        plan.append(((low, a, -1), ("second", 1), (low, a, -2)))
        sibling(zs, a, -1)
        steps.append((number, (n, len(plan))))
        last.append((n, low, a))
        n = len(plan)
        plan.append(((high, a, 1), ("second", -1), (high, a, 2)))
        sibling(zs, a, 1)
        steps.append((number + 1, (n, len(plan))))
        last.append((n, high, a))
    for number, zs, a in last:
        n = len(plan)
        sibling(zs, a, 2)
        steps.append((number, (n, len(plan))))
    return plan, marks, steps


PLAN, MARKS, STEPS = spread_plan()


def device(z, y, x, core):
    return {"zh": z // 8, "core": core, "zl": lax.rem(z, 8), "y": y, "x": x}


def split(value):
    high = value.astype(BF16).astype(F32)
    return jnp.concatenate([high, value - high], axis=0).astype(BF16)


def kernel(v_ref, diag_ref, shift_ref, rot_ref, mine_ref, cols_ref, out_ref,
           op, grid_v, grid_t, turn, zs_v, zs_t, zs_f, zs_g, zb_v, zb_t, zb_f, zb_g,
           xb, vc, rv, tb, fm, fsib, pm, psib, fr, pr, wf, wg, ib_f, ib_g, hf, eb,
           op_send, op_recv, op_local, plane_send, plane_recv, z_send, z_recv, pair_send, pair_recv):
    zh, core, zl = lax.axis_index("zh"), lax.axis_index("core"), lax.axis_index("zl")
    y, x = lax.axis_index("y"), lax.axis_index("x")
    z = zh * 8 + zl
    p = y * 4 + x

    def at_z(other):
        return device(other, y, x, core)

    def at_p(other):
        return {"zh": zh, "core": core, "zl": zl, "y": other // 4, "x": lax.rem(other, 4)}

    pair = {"zh": zh, "core": 1 - core, "zl": zl, "y": y, "x": x}

    energy = shift_ref[0]
    eb[zh] = jnp.full((8, 128), energy, F32)
    turn[...] = jnp.zeros_like(turn)
    barrier = pltpu.get_barrier_semaphore()

    @pl.loop(1, 16)
    def _(step):
        pl.semaphore_signal(barrier, inc=1, device_id=at_z(lax.rem(z + step, 16)), device_id_type=ONTO)
        pl.semaphore_signal(barrier, inc=1, device_id=at_p(lax.rem(p + step, 16)), device_id_type=ONTO)

    pl.semaphore_signal(barrier, inc=1, device_id=pair, device_id_type=ONTO)
    pl.semaphore_wait(barrier, 31)

    def plane_copy(kind, src, dst, to, source):
        return pltpu.make_async_remote_copy(
            src_ref=src, dst_ref=dst, send_sem=plane_send.at[kind, to], recv_sem=plane_recv.at[kind, source],
            device_id=at_p(to), device_id_type=ONTO)

    def z_copy(kind, src, dst, to, source):
        return pltpu.make_async_remote_copy(
            src_ref=src, dst_ref=dst, send_sem=z_send.at[kind, to], recv_sem=z_recv.at[kind, source],
            device_id=at_z(to), device_id_type=ONTO)

    def rows24(ref, index):
        return ref.at[pl.ds(pl.multiple_of(index * 24, 8), 24), :]

    def wait_plane(kind, slot):
        @pl.loop(1, 16)
        def _(step):
            other = lax.rem(p + step, 16)
            plane_copy(kind, slot(other), slot(other), other, other).wait_recv()

    def wait_z(kind, ref):
        @pl.loop(1, 16)
        def _(step):
            other = lax.rem(z + step, 16)
            z_copy(kind, ref.at[other], ref.at[other], other, other).wait_recv()

    def sent_plane(kind, slot):
        @pl.loop(1, 16)
        def _(step):
            other = lax.rem(p + step, 16)
            plane_copy(kind, slot(other), slot(other), other, other).wait_send()

    def sent_z(kind, ref):
        @pl.loop(1, 16)
        def _(step):
            other = lax.rem(z + step, 16)
            z_copy(kind, ref.at[other], ref.at[other], other, other).wait_send()

    def spread(color):
        rows = (0, CUT) if color == 0 else (CUT, 240 - CUT)
        others = (CUT, 240 - CUT) if color == 0 else (0, CUT)
        place = {"y": y, "x": x}

        def of(piece, part, first, second):
            zs, a, b = piece
            index = {first: lax.rem(place[first] + a + 4, 4), second: lax.rem(place[second] + b + 4, 4)}
            return op.at[pl.ds(zs[0], zs[1]), index["y"], index["x"], pl.ds(part[0], part[1])]

        first, second = ("y", "x") if color == 0 else ("x", "y")

        def copy(number, landing=False):
            piece, (axis, step), lands = PLAN[number]
            if piece == "z":
                source = lax.rem(zl - step + 8, 8) if landing else zl
                ref = op.at[source, y, x, pl.ds(rows[0], rows[1])]
                to = at_z(lax.rem(z + step + 16, 16))
            elif axis == "core":
                ref = of(piece, others, second, first) if landing else of(piece, rows, first, second)
                to = pair
            else:
                ref = of(lands if landing else piece, rows, first, second)
                name = first if axis == "first" else second
                there = dict(place)
                there[name] = lax.rem(place[name] + step + 4, 4)
                to = device(z, there["y"], there["x"], core)
            return pltpu.make_async_remote_copy(
                src_ref=ref, dst_ref=ref, send_sem=op_send.at[number], recv_sem=op_recv.at[number],
                device_id=to, device_id_type=ONTO)

        return rows, copy

    def by_color(body):
        for color in (0, 1):
            @pl.when(core == color)
            def _():
                body(*spread(color))

    def spread_start(rows, copy):
        part = pl.ds(rows[0], rows[1])
        own = pltpu.make_async_copy(mine_ref.at[part], op.at[zl, y, x, part], op_local)
        own.start()
        own.wait()
        for number in range(7):
            copy(number).start()

    def spread_on(rows, copy):
        for number in range(7):
            copy(number, True).wait_recv()
        for number in range(*MARKS["start"]):
            copy(number).start()

    def spread_rest(rows, copy):
        for number, (low, high) in STEPS:
            copy(number, True).wait_recv()
            for follow in range(low, high):
                copy(follow).start()
        for number in range(len(PLAN)):
            if PLAN[number][1][0] == "core":
                copy(number, True).wait_recv()

    def spread_sent(rows, copy):
        for number in range(len(PLAN)):
            copy(number).wait_send()

    def window(target):
        return pl.ds(pl.multiple_of((3 * (target // 2) + lax.rem(target, 2)) * 128, 128), 256)

    half = pl.ds(pl.multiple_of(lax.rem(p, 2) * 64, 64), 192)
    mine24 = pl.ds(pl.multiple_of(p * 24, 8), 24)

    def turn_rows(grid, zs):
        for k in range(3):
            rows = slice(128 * k, 128 * k + 128)
            turn[0:128, :] = grid[rows, 0:128].T
            turn[128:256, :] = grid[rows, 128:256].T
            columns = turn[half, :]
            for target in range(16):
                zs[target, 12 * k:12 * k + 12, :] = columns[12 * target:12 * target + 12]

    def send_z(kind, zs, zb, target):
        @pl.when(target != z)
        def _():
            z_copy(kind, zs.at[target], zb.at[z], target, z).start()

        @pl.when(target == z)
        def _():
            zb[z] = zs[z]

    def send_all_z(kind, zs, zb):
        @pl.loop(0, 16)
        def _(step):
            send_z(kind, zs, zb, lax.rem(z + 8 + step, 16))

    def turn_columns(zb, rows_out):
        for k in range(3):
            turn[half, :] = jnp.concatenate([zb[source, 12 * k:12 * k + 12, :] for source in range(16)], axis=0)
            rows = slice(128 * k, 128 * k + 128)
            rows_out[rows, 0:128] = turn[0:128, :].T
            rows_out[rows, 128:256] = turn[128:256, :].T

    def send_rows(kind, rows_out, ib):
        @pl.loop(1, 16)
        def _(step):
            target = lax.rem(p + step, 16)
            plane_copy(kind, rows24(rows_out, target), ib.at[p], target, p).start()

        ib[p] = rows_out[mine24, :]

    low_lanes = lax.broadcasted_iota(jnp.int32, (24, 128), 1) < 64

    def merged(ib, m):
        even, odd = ib[2 * m], ib[2 * m + 1]
        return even[:, 0:128], jnp.where(low_lanes, even[:, 128:256], odd[:, 0:128]), odd[:, 128:256]

    def block(m, ii, f):
        row = ii * 1280 + f * 128
        parts, left = [], 128
        while left:
            place, offset = divmod(row, 240)
            take = min(left, 240 - offset)
            parts.append(op[m, place // 4, place % 4, offset:offset + take, :])
            row, left = row + take, left - take
        return parts[0] if len(parts) == 1 else jnp.concatenate(parts, axis=0)

    def operate(first, emit, after=None):
        @pl.loop(0, 8)
        def _(step):
            m = lax.rem(first + step, 8)
            for ii in range(3):
                vectors = jnp.concatenate([xb[cols_ref[3 * m + ii, f]] for f in range(10)], axis=1)
                blocks = jnp.concatenate([block(m, ii, f) for f in range(10)], axis=1)
                both = lax.dot_general(vectors, blocks, (((1,), (1,)), ((), ())), preferred_element_type=F32)
                emit(m, ii, both[0:24] + both[24:48])
            if after is not None:
                after(m)

    def lanes(m, ii):
        return pl.ds(pl.multiple_of((3 * m + ii) * 128, 128), 128)

    @pl.loop(1, 16)
    def _(step):
        target = lax.rem(p + step, 16)
        plane_copy(0, v_ref.at[:, window(target)], grid_v.at[mine24, :], target, p).start()

    grid_v[mine24, :] = v_ref[:, window(p)]
    by_color(spread_start)
    energy_copy = pltpu.make_async_remote_copy(
        src_ref=eb.at[zh], dst_ref=eb.at[zh], send_sem=pair_send.at[2], recv_sem=pair_recv.at[2],
        device_id=at_z(lax.rem(z + 8, 16)), device_id_type=ONTO)
    energy_copy.start()

    @pl.loop(0, 8)
    def _(m):
        for ii in range(3):
            xb[3 * m + ii] = split(v_ref[:, lanes(m, ii)])

    by_color(spread_on)
    wait_plane(0, lambda other: rows24(grid_v, other))
    turn_rows(grid_v, zs_v)
    send_all_z(0, zs_v, zb_v)
    by_color(spread_rest)

    def emit_t(m, ii, value):
        here = lanes(m, ii)
        tb[m, :, 128 * ii:128 * ii + 128] = value + (diag_ref[:, here] - energy) * v_ref[:, here]

    def after_t(m):
        for odd in (0, 1):
            target = 2 * m + odd
            part = tb.at[m, :, pl.ds(128 * odd, 256)]

            @pl.when(target != p)
            def _():
                plane_copy(1, part, grid_t.at[mine24, :], target, p).start()

            @pl.when(target == p)
            def _():
                grid_t[mine24, :] = tb[m, :, 128 * odd:128 * odd + 256]

    operate(lax.rem(p // 2 + 1, 8), emit_t, after_t)

    wait_plane(1, lambda other: rows24(grid_t, other))
    turn_rows(grid_t, zs_t)
    send_all_z(1, zs_t, zb_t)

    wait_z(0, zb_v)

    @pl.loop(0, 8)
    def _(m):
        for k in range(3):
            part = slice(12 * k, 12 * k + 12)
            both = jnp.concatenate([zb_v[m, part, :], zb_v[8 + m, part, :]], axis=0)
            vc[3 * m + k] = both
            xb[3 * m + k] = split(both)

    def emit_rv(m, ii, value):
        rv[3 * m + ii] = value

    operate(0, emit_rv)
    wait_z(1, zb_t)

    other_energy = pltpu.make_async_remote_copy(
        src_ref=eb.at[1 - zh], dst_ref=eb.at[1 - zh], send_sem=pair_send.at[2], recv_sem=pair_recv.at[2],
        device_id=at_z(lax.rem(z + 8, 16)), device_id_type=ONTO)
    other_energy.wait_recv()
    upper = lax.broadcasted_iota(jnp.int32, (24, 128), 0) < 12
    shifts = jnp.where(upper, jnp.broadcast_to(eb[0, 0:1, :], (24, 128)), jnp.broadcast_to(eb[1, 0:1, :], (24, 128)))

    def weights(to_core):
        straight = jnp.where(upper, rot_ref[to_core, core], rot_ref[2 + to_core, 2 + core])
        crossed = jnp.where(upper, rot_ref[to_core, 2 + core], rot_ref[2 + to_core, core])
        return straight, crossed

    here_straight, here_crossed = weights(core)
    there_straight, there_crossed = weights(1 - core)

    def swapped(value):
        return jnp.concatenate([value[12:24], value[0:12]], axis=0)

    @pl.loop(0, 8)
    def _(m):
        for k in range(3):
            c = 3 * m + k
            part = slice(12 * k, 12 * k + 12)
            t = jnp.concatenate([zb_t[m, part, :], zb_t[8 + m, part, :]], axis=0)
            first = 0.5 * (rv[c] + t)
            turned = swapped(first)
            rest = shifts * first + vc[c]
            rest_turned = swapped(rest)
            fm[c] = here_straight * first + here_crossed * turned
            fsib[c] = there_straight * first + there_crossed * turned
            pm[c] = here_straight * rest + here_crossed * rest_turned
            psib[c] = there_straight * rest + there_crossed * rest_turned

    def pair_copy(index, src, dst):
        return pltpu.make_async_remote_copy(
            src_ref=src, dst_ref=dst, send_sem=pair_send.at[index], recv_sem=pair_recv.at[index],
            device_id=pair, device_id_type=ONTO)

    pair_copy(0, fsib, fr).start()
    pair_copy(1, psib, pr).start()
    pair_copy(0, fsib, fr).wait_recv()

    @pl.loop(0, 8)
    def _(step):
        m = lax.rem(zl + step, 8)
        for k in range(3):
            c = 3 * m + k
            value = fm[c] + fr[c]
            xb[c] = split(value)
            zs_f[m, 12 * k:12 * k + 12, :] = value[0:12]
            zs_f[8 + m, 12 * k:12 * k + 12, :] = value[12:24]
        send_z(2, zs_f, zb_f, m)
        send_z(2, zs_f, zb_f, m + 8)

    pair_copy(1, psib, pr).wait_recv()

    def emit_g(m, ii, value):
        c = 3 * m + ii
        g = value - (pm[c] + pr[c])
        zs_g[m, 12 * ii:12 * ii + 12, :] = g[0:12]
        zs_g[8 + m, 12 * ii:12 * ii + 12, :] = g[12:24]

    def after_g(m):
        send_z(3, zs_g, zb_g, m)
        send_z(3, zs_g, zb_g, m + 8)

    operate(zl, emit_g, after_g)

    wait_z(2, zb_f)
    turn_columns(zb_f, wf)
    send_rows(2, wf, ib_f)
    wait_plane(2, lambda other: ib_f.at[other])

    @pl.loop(0, 8)
    def _(m):
        for ii, tile in enumerate(merged(ib_f, m)):
            hf[m, :, 128 * ii:128 * ii + 128] = tile
            xb[3 * m + ii] = split(tile)

    def emit_out(m, ii, value):
        here = lanes(m, ii)
        out_ref[:, here] = value + diag_ref[:, here] * hf[m, :, 128 * ii:128 * ii + 128]

    operate(0, emit_out)
    wait_z(3, zb_g)
    turn_columns(zb_g, wg)
    send_rows(3, wg, ib_g)
    wait_plane(3, lambda other: ib_g.at[other])

    @pl.loop(0, 8)
    def _(m):
        for ii, tile in enumerate(merged(ib_g, m)):
            here = lanes(m, ii)
            out_ref[:, here] = out_ref[:, here] + tile

    by_color(spread_sent)
    energy_copy.wait_send()
    pair_copy(0, fsib, fr).wait_send()
    pair_copy(1, psib, pr).wait_send()
    sent_plane(0, lambda other: rows24(grid_v, other))
    sent_plane(1, lambda other: rows24(grid_t, other))
    sent_plane(2, lambda other: ib_f.at[other])
    sent_plane(3, lambda other: ib_g.at[other])
    for kind, ref in enumerate((zs_v, zs_t, zs_f, zs_g)):
        sent_z(kind, ref)


def shards(coeffs, diagonal, shift, rotation, string_blocks, block_cols):
    vmem = pl.BlockSpec(memory_space=pltpu.VMEM)
    smem = pl.BlockSpec(memory_space=pltpu.SMEM)
    grid = pltpu.VMEM((384, 256), F32)
    packed = pltpu.VMEM((16, 36, 128), F32)
    chunks = pltpu.VMEM((24, 24, 128), F32)
    windows = pltpu.VMEM((16, 24, 256), F32)
    wide = pltpu.VMEM((8, 24, 384), F32)
    dma = pltpu.SemaphoreType.DMA
    result = pl.pallas_call(
        kernel,
        out_shape=jax.ShapeDtypeStruct((24, 3072), F32),
        in_specs=[vmem, vmem, smem, smem, vmem, smem],
        out_specs=vmem,
        scratch_shapes=[
            pltpu.VMEM((8, 4, 4, 240, 128), BF16),
            grid, grid, pltpu.VMEM((256, 128), F32),
            packed, packed, packed, packed, packed, packed, packed, packed,
            pltpu.VMEM((24, 48, 128), BF16),
            chunks, chunks, wide,
            chunks, chunks, chunks, chunks, chunks, chunks,
            grid, grid, windows, windows, wide,
            pltpu.VMEM((2, 8, 128), F32),
            dma((len(PLAN),)), dma((len(PLAN),)), dma,
            dma((4, 16)), dma((4, 16)), dma((4, 16)), dma((4, 16)), dma((3,)), dma((3,)),
        ],
        compiler_params=pltpu.CompilerParams(
            collective_id=0, has_side_effects=True, vmem_limit_bytes=48 * 1024 * 1024),
        name="filter",
    )(coeffs[0], diagonal, shift, rotation, string_blocks, block_cols)
    return result[None]


def solution(mesh):
    split_mesh = Mesh(mesh.devices.reshape(2, 2, 8, 4, 4), ROOT + COL)
    return jax.shard_map(
        shards,
        mesh=split_mesh,
        in_specs=(P(ROOT, COL, None), P(COL, None), P(ROOT), P(), P(COL, None), P()),
        out_specs=P(ROOT, COL, None),
        check_vma=False,
    )
```

```python
import jax
import jax.numpy as jnp
from jax import lax
from jax.experimental import pallas as pl
from jax.experimental.pallas import tpu as pltpu
from jax.sharding import Mesh
from jax.sharding import PartitionSpec as P

ROOT = ("zh", "core")
COL = ("zl", "y", "x")
CUT = 128
F32, BF16 = jnp.float32, jnp.bfloat16
ONTO = pl.DeviceIdType.MESH

E, H, Q = (0, 8), ((0, 4), (4, 4)), ((0, 2), (2, 2), (4, 2), (6, 2))
Z_STEPS = (1, -1, 2, -2, 3, -3, 4)


def spread_plan():
    plan = [("z", ("z", d), None) for d in Z_STEPS]

    def both(zs, a):
        plan.append(((zs, a, 0), ("second", 1), (zs, a, -1)))
        plan.append(((zs, a, 0), ("second", -1), (zs, a, 1)))

    def sibling(zs, a, b):
        plan.append(((zs, a, b), ("core", 1), "sibling"))

    plan.append(((E, 0, 0), ("first", 1), (E, -1, 0)))
    plan.append(((E, 0, 0), ("first", -1), (E, 1, 0)))
    both(E, 0)
    sibling(E, 0, 0)
    marks = {"start": (7, 12)}
    steps = []
    n = len(plan)
    plan.append(((H[0], -1, 0), ("first", 1), (H[0], -2, 0)))
    both(E, -1)
    sibling(E, -1, 0)
    steps.append((7, (n, len(plan))))
    far_low = n
    n = len(plan)
    plan.append(((H[1], 1, 0), ("first", -1), (H[1], 2, 0)))
    both(E, 1)
    sibling(E, 1, 0)
    steps.append((8, (n, len(plan))))
    far_high = n
    n = len(plan)
    both(H[0], 2)
    sibling(H[0], 2, 0)
    steps.append((far_low, (n, len(plan))))
    n = len(plan)
    both(H[1], 2)
    sibling(H[1], 2, 0)
    steps.append((far_high, (n, len(plan))))
    sets = [(0, E, H[0], H[1], 9), (-1, E, H[0], H[1], 13), (1, E, H[0], H[1], 17),
            (2, H[0], Q[0], Q[1], 20), (2, H[1], Q[2], Q[3], 23)]
    last = []
    for a, zs, low, high, number in sets:
        n = len(plan)
        plan.append(((low, a, -1), ("second", 1), (low, a, -2)))
        sibling(zs, a, -1)
        steps.append((number, (n, len(plan))))
        last.append((n, low, a))
        n = len(plan)
        plan.append(((high, a, 1), ("second", -1), (high, a, 2)))
        sibling(zs, a, 1)
        steps.append((number + 1, (n, len(plan))))
        last.append((n, high, a))
    for number, zs, a in last:
        n = len(plan)
        sibling(zs, a, 2)
        steps.append((number, (n, len(plan))))
    return plan, marks, steps


PLAN, MARKS, STEPS = spread_plan()


def device(z, y, x, core):
    return {"zh": z // 8, "core": core, "zl": lax.rem(z, 8), "y": y, "x": x}


def split(value):
    high = value.astype(BF16).astype(F32)
    return jnp.concatenate([high, value - high], axis=0).astype(BF16)


def kernel(v_any, diag_any, shift_ref, rot_ref, mine_ref, cols_ref, out_ref,
           v_ref, diag_ref, op, grid_v, grid_t, turn, zs_v, zs_t, zs_f, zs_g, zb_v, zb_t, zb_f, zb_g,
           xb, vc, rv, tb, fm, fsib, pm, psib, fr, pr, wf, wg, ib_f, ib_g, hf, eb,
           op_send, op_recv, local, plane_send, plane_recv, z_send, z_recv, pair_send, pair_recv):
    zh, core, zl = lax.axis_index("zh"), lax.axis_index("core"), lax.axis_index("zl")
    y, x = lax.axis_index("y"), lax.axis_index("x")
    z = zh * 8 + zl
    p = y * 4 + x

    def at_z(other):
        return device(other, y, x, core)

    def at_p(other):
        return {"zh": zh, "core": core, "zl": zl, "y": other // 4, "x": lax.rem(other, 4)}

    pair = {"zh": zh, "core": 1 - core, "zl": zl, "y": y, "x": x}

    barrier = pltpu.get_barrier_semaphore()

    @pl.loop(1, 16)
    def _(step):
        pl.semaphore_signal(barrier, inc=1, device_id=at_z(lax.rem(z + step, 16)), device_id_type=ONTO)
        pl.semaphore_signal(barrier, inc=1, device_id=at_p(lax.rem(p + step, 16)), device_id_type=ONTO)

    pl.semaphore_signal(barrier, inc=1, device_id=pair, device_id_type=ONTO)
    load_v = pltpu.make_async_copy(v_any.at[0], v_ref, local.at[0])
    load_diag = pltpu.make_async_copy(diag_any, diag_ref, local.at[1])
    load_v.start()
    load_diag.start()

    @pl.when(core == 0)
    def _():
        part = pl.ds(0, CUT)
        load = pltpu.make_async_copy(mine_ref.at[part], op.at[zl, y, x, part], local.at[2])
        load.start()
        load.wait()

    @pl.when(core == 1)
    def _():
        part = pl.ds(CUT, 240 - CUT)
        load = pltpu.make_async_copy(mine_ref.at[part], op.at[zl, y, x, part], local.at[2])
        load.start()
        load.wait()

    energy = shift_ref[0]
    eb[zh] = jnp.full((8, 128), energy, F32)
    turn[...] = jnp.zeros_like(turn)
    load_v.wait()
    load_diag.wait()
    grid_v[pl.ds(pl.multiple_of(p * 24, 8), 24), :] = v_ref[
        :, pl.ds(pl.multiple_of((3 * (p // 2) + lax.rem(p, 2)) * 128, 128), 256)]

    @pl.loop(0, 24)
    def _(c):
        xb[c] = split(v_ref[:, pl.ds(pl.multiple_of(c * 128, 128), 128)])

    pl.semaphore_wait(barrier, 31)

    def plane_copy(kind, src, dst, to, source):
        return pltpu.make_async_remote_copy(
            src_ref=src, dst_ref=dst, send_sem=plane_send.at[kind, to], recv_sem=plane_recv.at[kind, source],
            device_id=at_p(to), device_id_type=ONTO)

    def z_copy(kind, src, dst, to, source):
        return pltpu.make_async_remote_copy(
            src_ref=src, dst_ref=dst, send_sem=z_send.at[kind, to], recv_sem=z_recv.at[kind, source],
            device_id=at_z(to), device_id_type=ONTO)

    def rows24(ref, index):
        return ref.at[pl.ds(pl.multiple_of(index * 24, 8), 24), :]

    def wait_plane(kind, slot):
        @pl.loop(1, 16)
        def _(step):
            other = lax.rem(p + step, 16)
            plane_copy(kind, slot(other), slot(other), other, other).wait_recv()

    def wait_z(kind, ref):
        @pl.loop(1, 16)
        def _(step):
            other = lax.rem(z + step, 16)
            z_copy(kind, ref.at[other], ref.at[other], other, other).wait_recv()

    def sent_plane(kind, slot):
        @pl.loop(1, 16)
        def _(step):
            other = lax.rem(p + step, 16)
            plane_copy(kind, slot(other), slot(other), other, other).wait_send()

    def sent_z(kind, ref):
        @pl.loop(1, 16)
        def _(step):
            other = lax.rem(z + step, 16)
            z_copy(kind, ref.at[other], ref.at[other], other, other).wait_send()

    def spread(color):
        rows = (0, CUT) if color == 0 else (CUT, 240 - CUT)
        others = (CUT, 240 - CUT) if color == 0 else (0, CUT)
        place = {"y": y, "x": x}

        def of(piece, part, first, second):
            zs, a, b = piece
            index = {first: lax.rem(place[first] + a + 4, 4), second: lax.rem(place[second] + b + 4, 4)}
            return op.at[pl.ds(zs[0], zs[1]), index["y"], index["x"], pl.ds(part[0], part[1])]

        first, second = ("y", "x") if color == 0 else ("x", "y")

        def copy(number, landing=False):
            piece, (axis, step), lands = PLAN[number]
            if piece == "z":
                source = lax.rem(zl - step + 8, 8) if landing else zl
                ref = op.at[source, y, x, pl.ds(rows[0], rows[1])]
                to = at_z(lax.rem(z + step + 16, 16))
            elif axis == "core":
                ref = of(piece, others, second, first) if landing else of(piece, rows, first, second)
                to = pair
            else:
                ref = of(lands if landing else piece, rows, first, second)
                name = first if axis == "first" else second
                there = dict(place)
                there[name] = lax.rem(place[name] + step + 4, 4)
                to = device(z, there["y"], there["x"], core)
            return pltpu.make_async_remote_copy(
                src_ref=ref, dst_ref=ref, send_sem=op_send.at[number], recv_sem=op_recv.at[number],
                device_id=to, device_id_type=ONTO)

        return rows, copy

    def by_color(body):
        for color in (0, 1):
            @pl.when(core == color)
            def _():
                body(*spread(color))

    def spread_start(rows, copy):
        for number in range(7):
            copy(number).start()

    def spread_on(rows, copy):
        for number in range(7):
            copy(number, True).wait_recv()
        for number in range(*MARKS["start"]):
            copy(number).start()

    def spread_rest(rows, copy):
        for number, (low, high) in STEPS:
            copy(number, True).wait_recv()
            for follow in range(low, high):
                copy(follow).start()
        for number in range(len(PLAN)):
            if PLAN[number][1][0] == "core":
                copy(number, True).wait_recv()

    def spread_sent(rows, copy):
        for number in range(len(PLAN)):
            copy(number).wait_send()

    def window(target):
        return pl.ds(pl.multiple_of((3 * (target // 2) + lax.rem(target, 2)) * 128, 128), 256)

    half = pl.ds(pl.multiple_of(lax.rem(p, 2) * 64, 64), 192)
    mine24 = pl.ds(pl.multiple_of(p * 24, 8), 24)

    def turn_rows(grid, zs):
        for k in range(3):
            rows = slice(128 * k, 128 * k + 128)
            turn[0:128, :] = grid[rows, 0:128].T
            turn[128:256, :] = grid[rows, 128:256].T
            columns = turn[half, :]
            for target in range(16):
                zs[target, 12 * k:12 * k + 12, :] = columns[12 * target:12 * target + 12]

    def send_z(kind, zs, zb, target):
        @pl.when(target != z)
        def _():
            z_copy(kind, zs.at[target], zb.at[z], target, z).start()

        @pl.when(target == z)
        def _():
            zb[z] = zs[z]

    def send_all_z(kind, zs, zb):
        @pl.loop(0, 16)
        def _(step):
            send_z(kind, zs, zb, lax.rem(z + 8 + step, 16))

    def turn_columns(zb, rows_out):
        for k in range(3):
            turn[half, :] = jnp.concatenate([zb[source, 12 * k:12 * k + 12, :] for source in range(16)], axis=0)
            rows = slice(128 * k, 128 * k + 128)
            rows_out[rows, 0:128] = turn[0:128, :].T
            rows_out[rows, 128:256] = turn[128:256, :].T

    def send_rows(kind, rows_out, ib):
        @pl.loop(1, 16)
        def _(step):
            target = lax.rem(p + step, 16)
            plane_copy(kind, rows24(rows_out, target), ib.at[p], target, p).start()

        ib[p] = rows_out[mine24, :]

    low_lanes = lax.broadcasted_iota(jnp.int32, (24, 128), 1) < 64

    def merged(ib, m):
        even, odd = ib[2 * m], ib[2 * m + 1]
        return even[:, 0:128], jnp.where(low_lanes, even[:, 128:256], odd[:, 0:128]), odd[:, 128:256]

    def block(m, ii, f):
        row = ii * 1280 + f * 128
        parts, left = [], 128
        while left:
            place, offset = divmod(row, 240)
            take = min(left, 240 - offset)
            parts.append(op[m, place // 4, place % 4, offset:offset + take, :])
            row, left = row + take, left - take
        return parts[0] if len(parts) == 1 else jnp.concatenate(parts, axis=0)

    def operate(first, emit, after=None):
        @pl.loop(0, 8)
        def _(step):
            m = lax.rem(first + step, 8)
            for ii in range(3):
                vectors = jnp.concatenate([xb[cols_ref[f, 3 * m + ii]] for f in range(10)], axis=1)
                blocks = jnp.concatenate([block(m, ii, f) for f in range(10)], axis=1)
                both = lax.dot_general(vectors, blocks, (((1,), (1,)), ((), ())), preferred_element_type=F32)
                emit(m, ii, both[0:24] + both[24:48])
            if after is not None:
                after(m)

    def lanes(m, ii):
        return pl.ds(pl.multiple_of((3 * m + ii) * 128, 128), 128)

    by_color(spread_start)

    @pl.loop(1, 16)
    def _(step):
        target = lax.rem(p + step, 16)
        plane_copy(0, v_ref.at[:, window(target)], grid_v.at[mine24, :], target, p).start()

    energy_copy = pltpu.make_async_remote_copy(
        src_ref=eb.at[zh], dst_ref=eb.at[zh], send_sem=pair_send.at[2], recv_sem=pair_recv.at[2],
        device_id=at_z(lax.rem(z + 8, 16)), device_id_type=ONTO)
    energy_copy.start()

    by_color(spread_on)
    wait_plane(0, lambda other: rows24(grid_v, other))
    turn_rows(grid_v, zs_v)
    send_all_z(0, zs_v, zb_v)
    by_color(spread_rest)

    def emit_t(m, ii, value):
        here = lanes(m, ii)
        tb[m, :, 128 * ii:128 * ii + 128] = value + (diag_ref[:, here] - energy) * v_ref[:, here]

    def after_t(m):
        for odd in (0, 1):
            target = 2 * m + odd
            part = tb.at[m, :, pl.ds(128 * odd, 256)]

            @pl.when(target != p)
            def _():
                plane_copy(1, part, grid_t.at[mine24, :], target, p).start()

            @pl.when(target == p)
            def _():
                grid_t[mine24, :] = tb[m, :, 128 * odd:128 * odd + 256]

    operate(lax.rem(p // 2 + 1, 8), emit_t, after_t)

    wait_plane(1, lambda other: rows24(grid_t, other))
    turn_rows(grid_t, zs_t)
    send_all_z(1, zs_t, zb_t)

    wait_z(0, zb_v)

    @pl.loop(0, 8)
    def _(m):
        for k in range(3):
            part = slice(12 * k, 12 * k + 12)
            both = jnp.concatenate([zb_v[m, part, :], zb_v[8 + m, part, :]], axis=0)
            vc[3 * m + k] = both
            xb[3 * m + k] = split(both)

    def emit_rv(m, ii, value):
        rv[3 * m + ii] = value

    operate(0, emit_rv)
    wait_z(1, zb_t)

    other_energy = pltpu.make_async_remote_copy(
        src_ref=eb.at[1 - zh], dst_ref=eb.at[1 - zh], send_sem=pair_send.at[2], recv_sem=pair_recv.at[2],
        device_id=at_z(lax.rem(z + 8, 16)), device_id_type=ONTO)
    other_energy.wait_recv()
    upper = lax.broadcasted_iota(jnp.int32, (24, 128), 0) < 12
    shifts = jnp.where(upper, jnp.broadcast_to(eb[0, 0:1, :], (24, 128)), jnp.broadcast_to(eb[1, 0:1, :], (24, 128)))

    def weights(to_core):
        straight = jnp.where(upper, rot_ref[to_core, core], rot_ref[2 + to_core, 2 + core])
        crossed = jnp.where(upper, rot_ref[to_core, 2 + core], rot_ref[2 + to_core, core])
        return straight, crossed

    here_straight, here_crossed = weights(core)
    there_straight, there_crossed = weights(1 - core)

    def swapped(value):
        return jnp.concatenate([value[12:24], value[0:12]], axis=0)

    @pl.loop(0, 8)
    def _(m):
        for k in range(3):
            c = 3 * m + k
            part = slice(12 * k, 12 * k + 12)
            t = jnp.concatenate([zb_t[m, part, :], zb_t[8 + m, part, :]], axis=0)
            first = 0.5 * (rv[c] + t)
            turned = swapped(first)
            rest = shifts * first + vc[c]
            rest_turned = swapped(rest)
            fm[c] = here_straight * first + here_crossed * turned
            fsib[c] = there_straight * first + there_crossed * turned
            pm[c] = here_straight * rest + here_crossed * rest_turned
            psib[c] = there_straight * rest + there_crossed * rest_turned

    def pair_copy(index, src, dst):
        return pltpu.make_async_remote_copy(
            src_ref=src, dst_ref=dst, send_sem=pair_send.at[index], recv_sem=pair_recv.at[index],
            device_id=pair, device_id_type=ONTO)

    pair_copy(0, fsib, fr).start()
    pair_copy(1, psib, pr).start()
    pair_copy(0, fsib, fr).wait_recv()

    @pl.loop(0, 8)
    def _(step):
        m = lax.rem(zl + step, 8)
        for k in range(3):
            c = 3 * m + k
            value = fm[c] + fr[c]
            xb[c] = split(value)
            zs_f[m, 12 * k:12 * k + 12, :] = value[0:12]
            zs_f[8 + m, 12 * k:12 * k + 12, :] = value[12:24]
        send_z(2, zs_f, zb_f, m)
        send_z(2, zs_f, zb_f, m + 8)

    pair_copy(1, psib, pr).wait_recv()

    def emit_g(m, ii, value):
        c = 3 * m + ii
        g = value - (pm[c] + pr[c])
        zs_g[m, 12 * ii:12 * ii + 12, :] = g[0:12]
        zs_g[8 + m, 12 * ii:12 * ii + 12, :] = g[12:24]

    def after_g(m):
        send_z(3, zs_g, zb_g, m)
        send_z(3, zs_g, zb_g, m + 8)

    operate(zl, emit_g, after_g)

    wait_z(2, zb_f)
    turn_columns(zb_f, wf)
    send_rows(2, wf, ib_f)
    wait_plane(2, lambda other: ib_f.at[other])

    @pl.loop(0, 8)
    def _(m):
        for ii, tile in enumerate(merged(ib_f, m)):
            hf[m, :, 128 * ii:128 * ii + 128] = tile
            xb[3 * m + ii] = split(tile)

    def emit_out(m, ii, value):
        here = lanes(m, ii)
        out_ref[:, here] = value + diag_ref[:, here] * hf[m, :, 128 * ii:128 * ii + 128]

    operate(0, emit_out)
    wait_z(3, zb_g)
    turn_columns(zb_g, wg)
    send_rows(3, wg, ib_g)
    wait_plane(3, lambda other: ib_g.at[other])

    @pl.loop(0, 8)
    def _(m):
        for ii, tile in enumerate(merged(ib_g, m)):
            here = lanes(m, ii)
            out_ref[:, here] = out_ref[:, here] + tile

    by_color(spread_sent)
    energy_copy.wait_send()
    pair_copy(0, fsib, fr).wait_send()
    pair_copy(1, psib, pr).wait_send()
    sent_plane(0, lambda other: rows24(grid_v, other))
    sent_plane(1, lambda other: rows24(grid_t, other))
    sent_plane(2, lambda other: ib_f.at[other])
    sent_plane(3, lambda other: ib_g.at[other])
    for kind, ref in enumerate((zs_v, zs_t, zs_f, zs_g)):
        sent_z(kind, ref)


def shards(coeffs, diagonal, shift, rotation, string_blocks, block_cols):
    vmem = pl.BlockSpec(memory_space=pltpu.VMEM)
    smem = pl.BlockSpec(memory_space=pltpu.SMEM)
    hbm = pl.BlockSpec(memory_space=pltpu.HBM)
    rows = pltpu.VMEM((24, 3072), F32)
    grid = pltpu.VMEM((384, 256), F32)
    packed = pltpu.VMEM((16, 36, 128), F32)
    chunks = pltpu.VMEM((24, 24, 128), F32)
    windows = pltpu.VMEM((16, 24, 256), F32)
    wide = pltpu.VMEM((8, 24, 384), F32)
    dma = pltpu.SemaphoreType.DMA
    result = pl.pallas_call(
        kernel,
        out_shape=jax.ShapeDtypeStruct((24, 3072), F32),
        in_specs=[hbm, hbm, smem, smem, hbm, smem],
        out_specs=vmem,
        scratch_shapes=[
            rows, rows, pltpu.VMEM((8, 4, 4, 240, 128), BF16),
            grid, grid, pltpu.VMEM((256, 128), F32),
            packed, packed, packed, packed, packed, packed, packed, packed,
            pltpu.VMEM((24, 48, 128), BF16),
            chunks, chunks, wide,
            chunks, chunks, chunks, chunks, chunks, chunks,
            grid, grid, windows, windows, wide,
            pltpu.VMEM((2, 8, 128), F32),
            dma((len(PLAN),)), dma((len(PLAN),)), dma((3,)),
            dma((4, 16)), dma((4, 16)), dma((4, 16)), dma((4, 16)), dma((3,)), dma((3,)),
        ],
        compiler_params=pltpu.CompilerParams(
            collective_id=0, has_side_effects=True, vmem_limit_bytes=48 * 1024 * 1024),
        name="filter",
    )(coeffs, diagonal, shift, rotation, string_blocks, block_cols.T)
    return result[None]


def solution(mesh):
    split_mesh = Mesh(mesh.devices.reshape(2, 2, 8, 4, 4), ROOT + COL)
    return jax.shard_map(
        shards,
        mesh=split_mesh,
        in_specs=(P(ROOT, COL, None), P(COL, None), P(ROOT), P(), P(COL, None), P()),
        out_specs=P(ROOT, COL, None),
        check_vma=False,
    )
```

```python
import jax
import jax.numpy as jnp
from jax import lax
from jax.experimental import pallas as pl
from jax.experimental.pallas import tpu as pltpu
from jax.sharding import Mesh
from jax.sharding import PartitionSpec as P

ROOT = ("zh", "core")
COL = ("zl", "y", "x")
CUT = 128
PARTS = (((0, 96), (96, 32)), ((CUT, 80), (CUT + 80, 32)))
F32, BF16 = jnp.float32, jnp.bfloat16
ONTO = pl.DeviceIdType.MESH

E, H, Q = (0, 8), ((0, 4), (4, 4)), ((0, 2), (2, 2), (4, 2), (6, 2))
Z_STEPS = (1, -1, 2, -2, 3, -3, 4)


def spread_plan():
    plan = [("z", ("z", d), None) for d in Z_STEPS]

    def both(zs, a):
        plan.append(((zs, a, 0), ("second", 1), (zs, a, -1)))
        plan.append(((zs, a, 0), ("second", -1), (zs, a, 1)))

    def sibling(zs, a, b):
        plan.append(((zs, a, b), ("core", 1), "sibling"))

    plan.append(((E, 0, 0), ("first", 1), (E, -1, 0)))
    plan.append(((E, 0, 0), ("first", -1), (E, 1, 0)))
    both(E, 0)
    sibling(E, 0, 0)
    marks = {"start": (7, 12)}
    steps = []
    n = len(plan)
    plan.append(((H[0], -1, 0), ("first", 1), (H[0], -2, 0)))
    both(E, -1)
    sibling(E, -1, 0)
    steps.append((7, (n, len(plan))))
    far_low = n
    n = len(plan)
    plan.append(((H[1], 1, 0), ("first", -1), (H[1], 2, 0)))
    both(E, 1)
    sibling(E, 1, 0)
    steps.append((8, (n, len(plan))))
    far_high = n
    n = len(plan)
    both(H[0], 2)
    sibling(H[0], 2, 0)
    steps.append((far_low, (n, len(plan))))
    n = len(plan)
    both(H[1], 2)
    sibling(H[1], 2, 0)
    steps.append((far_high, (n, len(plan))))
    sets = [(0, E, H[0], H[1], 9), (-1, E, H[0], H[1], 13), (1, E, H[0], H[1], 17),
            (2, H[0], Q[0], Q[1], 20), (2, H[1], Q[2], Q[3], 23)]
    last = []
    for a, zs, low, high, number in sets:
        n = len(plan)
        plan.append(((low, a, -1), ("second", 1), (low, a, -2)))
        sibling(zs, a, -1)
        steps.append((number, (n, len(plan))))
        last.append((n, low, a))
        n = len(plan)
        plan.append(((high, a, 1), ("second", -1), (high, a, 2)))
        sibling(zs, a, 1)
        steps.append((number + 1, (n, len(plan))))
        last.append((n, high, a))
    lasts = []
    for number, zs, a in last:
        n = len(plan)
        sibling(zs, a, 2)
        lasts.append((number, (n, len(plan))))

    def ring(part, half, way):
        plan.append((("ring", part, half), ("z", way), ("ring", part - way, half)))
        return len(plan) - 1

    def ring_sibling(part, half=None):
        plan.append((("ring", part, half), ("core", 1), "sibling"))

    n = len(plan)
    up, down = ring(0, None, 1), ring(0, None, -1)
    ring_sibling(0)
    marks["ring"] = (n, len(plan))
    rings = []
    for hop in (1, 2, 3):
        n = len(plan)
        next_up = ring(-hop, 0 if hop == 3 else None, 1)
        ring_sibling(-hop)
        rings.append((up, (n, len(plan))))
        n = len(plan)
        next_down = ring(hop, 1 if hop == 3 else None, -1)
        ring_sibling(hop)
        rings.append((down, (n, len(plan))))
        up, down = next_up, next_down
    for number, part, half in ((up, -4, 0), (down, 4, 1)):
        n = len(plan)
        ring_sibling(part, half)
        rings.append((number, (n, len(plan))))
    early = steps[0:2] + rings[0:2] + steps[2:8] + rings[2:4] + steps[8:12] + rings[4:6]
    late = steps[12:] + lasts + rings[6:8]
    return plan, marks, early, late


PLAN, MARKS, EARLY, LATE = spread_plan()


def device(z, y, x, core):
    return {"zh": z // 8, "core": core, "zl": lax.rem(z, 8), "y": y, "x": x}


def split(value):
    high = value.astype(BF16).astype(F32)
    return jnp.concatenate([high, value - high], axis=0).astype(BF16)


def kernel(v_any, diag_any, shift_ref, rot_ref, mine_ref, cols_ref, out_ref,
           v_ref, diag_ref, op, grid_v, grid_t, turn, zs_v, zs_t, zs_f, zs_g, zb_v, zb_t, zb_f, zb_g,
           sent_v, sent_t, sent_f, sent_g, got_v, got_t, got_f, got_g,
           xb, vc, rv, tb, fm, fsib, pm, psib, fr, pr, wf, wg, ib_f, ib_g, hf, eb,
           op_send, op_recv, local, plane_send, plane_recv, z_send, z_recv, pair_send, pair_recv):
    zh, core, zl = lax.axis_index("zh"), lax.axis_index("core"), lax.axis_index("zl")
    y, x = lax.axis_index("y"), lax.axis_index("x")
    z = zh * 8 + zl
    p = y * 4 + x

    def at_z(other):
        return device(other, y, x, core)

    def at_p(other):
        return {"zh": zh, "core": core, "zl": zl, "y": other // 4, "x": lax.rem(other, 4)}

    pair = {"zh": zh, "core": 1 - core, "zl": zl, "y": y, "x": x}

    barrier = pltpu.get_barrier_semaphore()

    @pl.loop(1, 16)
    def _(step):
        pl.semaphore_signal(barrier, inc=1, device_id=at_z(lax.rem(z + step, 16)), device_id_type=ONTO)
        pl.semaphore_signal(barrier, inc=1, device_id=at_p(lax.rem(p + step, 16)), device_id_type=ONTO)

    pl.semaphore_signal(barrier, inc=1, device_id=pair, device_id_type=ONTO)
    load_v = pltpu.make_async_copy(v_any.at[0], v_ref, local.at[0])
    load_diag = pltpu.make_async_copy(diag_any, diag_ref, local.at[1])
    load_v.start()
    load_diag.start()

    @pl.when(core == 0)
    def _():
        part = pl.ds(0, CUT)
        load = pltpu.make_async_copy(mine_ref.at[part], op.at[zl, y, x, part], local.at[2])
        load.start()
        load.wait()

    @pl.when(core == 1)
    def _():
        part = pl.ds(CUT, 240 - CUT)
        load = pltpu.make_async_copy(mine_ref.at[part], op.at[zl, y, x, part], local.at[2])
        load.start()
        load.wait()

    energy = shift_ref[0]
    eb[zh] = jnp.full((8, 128), energy, F32)
    turn[...] = jnp.zeros_like(turn)
    load_v.wait()
    load_diag.wait()
    grid_v[pl.ds(pl.multiple_of(p * 24, 8), 24), :] = v_ref[
        :, pl.ds(pl.multiple_of((3 * (p // 2) + lax.rem(p, 2)) * 128, 128), 256)]

    @pl.loop(0, 24)
    def _(c):
        xb[c] = split(v_ref[:, pl.ds(pl.multiple_of(c * 128, 128), 128)])

    pl.semaphore_wait(barrier, 31)

    def plane_copy(kind, src, dst, to, source):
        return pltpu.make_async_remote_copy(
            src_ref=src, dst_ref=dst, send_sem=plane_send.at[kind, to], recv_sem=plane_recv.at[kind, source],
            device_id=at_p(to), device_id_type=ONTO)

    def z_copy(kind, src, dst, to, source):
        return pltpu.make_async_remote_copy(
            src_ref=src, dst_ref=dst, send_sem=z_send.at[kind, to], recv_sem=z_recv.at[kind, source],
            device_id=at_z(to), device_id_type=ONTO)

    def rows24(ref, index):
        return ref.at[pl.ds(pl.multiple_of(index * 24, 8), 24), :]

    def wait_plane(kind, slot):
        @pl.loop(1, 16)
        def _(step):
            other = lax.rem(p + step, 16)
            plane_copy(kind, slot(other), slot(other), other, other).wait_recv()

    def wait_z(kind, ref):
        @pl.loop(1, 16)
        def _(step):
            other = lax.rem(z + step, 16)
            z_copy(kind, ref.at[other], ref.at[other], other, other).wait_recv()

    def sent_plane(kind, slot):
        @pl.loop(1, 16)
        def _(step):
            other = lax.rem(p + step, 16)
            plane_copy(kind, slot(other), slot(other), other, other).wait_send()

    def sent_z(kind, ref):
        @pl.loop(1, 16)
        def _(step):
            other = lax.rem(z + step, 16)
            z_copy(kind, ref.at[other], ref.at[other], other, other).wait_send()

    def spread(color):
        rows, around = PARTS[color]
        others, others_around = PARTS[1 - color]
        place = {"y": y, "x": x}

        def of(piece, part, first, second):
            zs, a, b = piece
            if zs == "ring":
                which = pl.ds(0, 4) if b is None else pl.ds(2 * b, 2)
                return op.at[lax.rem(zl + a + 8, 8), which, :, pl.ds(part[0], part[1])]
            index = {first: lax.rem(place[first] + a + 4, 4), second: lax.rem(place[second] + b + 4, 4)}
            return op.at[pl.ds(zs[0], zs[1]), index["y"], index["x"], pl.ds(part[0], part[1])]

        first, second = ("y", "x") if color == 0 else ("x", "y")

        def copy(number, landing=False):
            piece, (axis, step), lands = PLAN[number]
            if piece == "z":
                source = lax.rem(zl - step + 8, 8) if landing else zl
                ref = op.at[source, y, x, pl.ds(rows[0], rows[1])]
                to = at_z(lax.rem(z + step + 16, 16))
            elif axis == "core":
                going = around if piece[0] == "ring" else rows
                coming = others_around if piece[0] == "ring" else others
                ref = of(piece, coming, second, first) if landing else of(piece, going, first, second)
                to = pair
            elif axis == "z":
                ref = of(lands if landing else piece, around, first, second)
                to = at_z(lax.rem(z + step + 16, 16))
            else:
                ref = of(lands if landing else piece, rows, first, second)
                name = first if axis == "first" else second
                there = dict(place)
                there[name] = lax.rem(place[name] + step + 4, 4)
                to = device(z, there["y"], there["x"], core)
            return pltpu.make_async_remote_copy(
                src_ref=ref, dst_ref=ref, send_sem=op_send.at[number], recv_sem=op_recv.at[number],
                device_id=to, device_id_type=ONTO)

        return around, copy

    def by_color(body):
        for color in (0, 1):
            @pl.when(core == color)
            def _():
                body(*spread(color))

    def spread_start(around, copy):
        for number in range(7):
            copy(number).start()

        @pl.loop(1, 16)
        def _(step):
            target = lax.rem(p + step, 16)
            around_copy(around, p, target, p).start()

    def around_copy(around, source_slot, to, source):
        ref = op.at[zl, source_slot // 4, lax.rem(source_slot, 4), pl.ds(around[0], around[1])]
        return plane_copy(4, ref, ref, to, source)

    def spread_on(around, copy):
        for number in range(7):
            copy(number, True).wait_recv()
        for number in range(*MARKS["start"]):
            copy(number).start()

        @pl.loop(1, 16)
        def _(step):
            other = lax.rem(p + step, 16)
            around_copy(around, other, other, other).wait_recv()

        for number in range(*MARKS["ring"]):
            copy(number).start()
        follow_on(EARLY[:4], copy)

    def follow_on(steps, copy):
        for number, (low, high) in steps:
            copy(number, True).wait_recv()
            for follow in range(low, high):
                copy(follow).start()

    def spread_rest(around, copy):
        follow_on(EARLY[4:] + LATE, copy)
        for number in range(len(PLAN)):
            if PLAN[number][1][0] == "core":
                copy(number, True).wait_recv()

    def spread_sent(around, copy):
        for number in range(len(PLAN)):
            copy(number).wait_send()

        @pl.loop(1, 16)
        def _(step):
            other = lax.rem(p + step, 16)
            around_copy(around, p, other, other).wait_send()

    def window(target):
        return pl.ds(pl.multiple_of((3 * (target // 2) + lax.rem(target, 2)) * 128, 128), 256)

    half = pl.ds(pl.multiple_of(lax.rem(p, 2) * 64, 64), 192)
    mine24 = pl.ds(pl.multiple_of(p * 24, 8), 24)

    def turn_rows(grid, zs):
        for k in range(3):
            rows = slice(128 * k, 128 * k + 128)
            turn[0:128, :] = grid[rows, 0:128].T
            turn[128:256, :] = grid[rows, 128:256].T
            columns = turn[half, :]
            for target in range(16):
                zs[target, 12 * k:12 * k + 12, :] = columns[12 * target:12 * target + 12]

    own_lane = lax.broadcasted_iota(jnp.int32, (36, 128), 0) == lax.broadcasted_iota(jnp.int32, (36, 128), 1)

    def encode(zs, codes, target):
        value = zs[target]
        top = jnp.maximum(jnp.max(jnp.abs(value), axis=1, keepdims=True), 1e-30)
        level = jnp.ceil(jnp.log2(top) * 128.0)
        scaled = jnp.round(value * (jnp.exp2(level * (-1.0 / 128.0)) * 32700.0))
        levels = jnp.sum(jnp.where(own_lane, level, 0.0), axis=0, keepdims=True)
        whole = jnp.concatenate([scaled, jnp.broadcast_to(levels, (4, 128))], axis=0)
        codes[target] = whole.astype(jnp.int32).astype(jnp.int16)

    def decode(codes, zb):
        @pl.loop(0, 4)
        def _(quarter):
            for one in range(4):
                source = quarter * 4 + one
                whole = codes[source].astype(jnp.int32).astype(F32)
                levels = jnp.broadcast_to(whole[36:37], (36, 128))
                level = jnp.sum(jnp.where(own_lane, levels, 0.0), axis=1, keepdims=True)
                zb[source] = whole[0:36] * (jnp.exp2(level * (1.0 / 128.0)) * (1.0 / 32700.0))

    def send_z(kind, zs, zb, target):
        @pl.when(target != z)
        def _():
            z_copy(kind, zs.at[target], zb.at[z], target, z).start()

        @pl.when(target == z)
        def _():
            zb[z] = zs[z]

    def send_all_z(kind, zs, codes, landing):
        @pl.loop(0, 4)
        def _(step):
            group = [lax.rem(z + 8 + 4 * step + one, 16) for one in range(4)]
            for target in group:
                encode(zs, codes, target)
            for target in group:
                send_z(kind, codes, landing, target)

    def turn_columns(zb, rows_out):
        for k in range(3):
            turn[half, :] = jnp.concatenate([zb[source, 12 * k:12 * k + 12, :] for source in range(16)], axis=0)
            rows = slice(128 * k, 128 * k + 128)
            rows_out[rows, 0:128] = turn[0:128, :].T
            rows_out[rows, 128:256] = turn[128:256, :].T

    def send_rows(kind, rows_out, ib):
        @pl.loop(1, 16)
        def _(step):
            target = lax.rem(p + step, 16)
            plane_copy(kind, rows24(rows_out, target), ib.at[p], target, p).start()

        ib[p] = rows_out[mine24, :]

    low_lanes = lax.broadcasted_iota(jnp.int32, (24, 128), 1) < 64

    def merged(ib, m):
        even, odd = ib[2 * m], ib[2 * m + 1]
        return even[:, 0:128], jnp.where(low_lanes, even[:, 128:256], odd[:, 0:128]), odd[:, 128:256]

    def block(m, ii, f):
        row = ii * 1280 + f * 128
        parts, left = [], 128
        while left:
            place, offset = divmod(row, 240)
            take = min(left, 240 - offset)
            parts.append(op[m, place // 4, place % 4, offset:offset + take, :])
            row, left = row + take, left - take
        return parts[0] if len(parts) == 1 else jnp.concatenate(parts, axis=0)

    def operate(first, emit, after=None):
        @pl.loop(0, 8)
        def _(step):
            m = lax.rem(first + step, 8)
            for ii in range(3):
                vectors = jnp.concatenate([xb[cols_ref[f, 3 * m + ii]] for f in range(10)], axis=1)
                blocks = jnp.concatenate([block(m, ii, f) for f in range(10)], axis=1)
                both = lax.dot_general(vectors, blocks, (((1,), (1,)), ((), ())), preferred_element_type=F32)
                emit(m, ii, both[0:24] + both[24:48])
            if after is not None:
                after(m)

    def lanes(m, ii):
        return pl.ds(pl.multiple_of((3 * m + ii) * 128, 128), 128)

    by_color(spread_start)

    @pl.loop(1, 16)
    def _(step):
        target = lax.rem(p + step, 16)
        plane_copy(0, v_ref.at[:, window(target)], grid_v.at[mine24, :], target, p).start()

    energy_copy = pltpu.make_async_remote_copy(
        src_ref=eb.at[zh], dst_ref=eb.at[zh], send_sem=pair_send.at[2], recv_sem=pair_recv.at[2],
        device_id=at_z(lax.rem(z + 8, 16)), device_id_type=ONTO)
    energy_copy.start()

    by_color(spread_on)
    wait_plane(0, lambda other: rows24(grid_v, other))
    turn_rows(grid_v, zs_v)
    send_all_z(0, zs_v, sent_v, got_v)
    by_color(spread_rest)

    def emit_t(m, ii, value):
        here = lanes(m, ii)
        tb[m, :, 128 * ii:128 * ii + 128] = value + (diag_ref[:, here] - energy) * v_ref[:, here]

    def after_t(m):
        for odd in (0, 1):
            target = 2 * m + odd
            part = tb.at[m, :, pl.ds(128 * odd, 256)]

            @pl.when(target != p)
            def _():
                plane_copy(1, part, grid_t.at[mine24, :], target, p).start()

            @pl.when(target == p)
            def _():
                grid_t[mine24, :] = tb[m, :, 128 * odd:128 * odd + 256]

    operate(lax.rem(p // 2 + 1, 8), emit_t, after_t)

    wait_plane(1, lambda other: rows24(grid_t, other))
    turn_rows(grid_t, zs_t)
    send_all_z(1, zs_t, sent_t, got_t)

    wait_z(0, got_v)
    decode(got_v, zb_v)

    @pl.loop(0, 8)
    def _(m):
        for k in range(3):
            part = slice(12 * k, 12 * k + 12)
            both = jnp.concatenate([zb_v[m, part, :], zb_v[8 + m, part, :]], axis=0)
            vc[3 * m + k] = both
            xb[3 * m + k] = split(both)

    def emit_rv(m, ii, value):
        rv[3 * m + ii] = value

    operate(0, emit_rv)
    wait_z(1, got_t)
    decode(got_t, zb_t)

    other_energy = pltpu.make_async_remote_copy(
        src_ref=eb.at[1 - zh], dst_ref=eb.at[1 - zh], send_sem=pair_send.at[2], recv_sem=pair_recv.at[2],
        device_id=at_z(lax.rem(z + 8, 16)), device_id_type=ONTO)
    other_energy.wait_recv()
    upper = lax.broadcasted_iota(jnp.int32, (24, 128), 0) < 12
    shifts = jnp.where(upper, jnp.broadcast_to(eb[0, 0:1, :], (24, 128)), jnp.broadcast_to(eb[1, 0:1, :], (24, 128)))

    def weights(to_core):
        straight = jnp.where(upper, rot_ref[to_core, core], rot_ref[2 + to_core, 2 + core])
        crossed = jnp.where(upper, rot_ref[to_core, 2 + core], rot_ref[2 + to_core, core])
        return straight, crossed

    here_straight, here_crossed = weights(core)
    there_straight, there_crossed = weights(1 - core)

    def swapped(value):
        return jnp.concatenate([value[12:24], value[0:12]], axis=0)

    @pl.loop(0, 8)
    def _(m):
        for k in range(3):
            c = 3 * m + k
            part = slice(12 * k, 12 * k + 12)
            t = jnp.concatenate([zb_t[m, part, :], zb_t[8 + m, part, :]], axis=0)
            first = 0.5 * (rv[c] + t)
            turned = swapped(first)
            rest = shifts * first + vc[c]
            rest_turned = swapped(rest)
            fm[c] = here_straight * first + here_crossed * turned
            fsib[c] = there_straight * first + there_crossed * turned
            pm[c] = here_straight * rest + here_crossed * rest_turned
            psib[c] = there_straight * rest + there_crossed * rest_turned

    def pair_copy(index, src, dst):
        return pltpu.make_async_remote_copy(
            src_ref=src, dst_ref=dst, send_sem=pair_send.at[index], recv_sem=pair_recv.at[index],
            device_id=pair, device_id_type=ONTO)

    pair_copy(0, fsib, fr).start()
    pair_copy(1, psib, pr).start()
    pair_copy(0, fsib, fr).wait_recv()

    @pl.loop(0, 8)
    def _(step):
        m = lax.rem(zl + step, 8)
        for k in range(3):
            c = 3 * m + k
            value = fm[c] + fr[c]
            xb[c] = split(value)
            zs_f[m, 12 * k:12 * k + 12, :] = value[0:12]
            zs_f[8 + m, 12 * k:12 * k + 12, :] = value[12:24]
        encode(zs_f, sent_f, m)
        encode(zs_f, sent_f, m + 8)
        send_z(2, sent_f, got_f, m)
        send_z(2, sent_f, got_f, m + 8)

    pair_copy(1, psib, pr).wait_recv()

    def emit_g(m, ii, value):
        c = 3 * m + ii
        g = value - (pm[c] + pr[c])
        zs_g[m, 12 * ii:12 * ii + 12, :] = g[0:12]
        zs_g[8 + m, 12 * ii:12 * ii + 12, :] = g[12:24]

    def after_g(m):
        encode(zs_g, sent_g, m)
        encode(zs_g, sent_g, m + 8)
        send_z(3, sent_g, got_g, m)
        send_z(3, sent_g, got_g, m + 8)

    operate(zl, emit_g, after_g)

    wait_z(2, got_f)
    decode(got_f, zb_f)
    turn_columns(zb_f, wf)
    send_rows(2, wf, ib_f)
    wait_z(3, got_g)
    decode(got_g, zb_g)
    turn_columns(zb_g, wg)
    send_rows(3, wg, ib_g)
    wait_plane(2, lambda other: ib_f.at[other])

    @pl.loop(0, 8)
    def _(m):
        for ii, tile in enumerate(merged(ib_f, m)):
            hf[m, :, 128 * ii:128 * ii + 128] = tile
            xb[3 * m + ii] = split(tile)

    def emit_out(m, ii, value):
        here = lanes(m, ii)
        out_ref[:, here] = value + diag_ref[:, here] * hf[m, :, 128 * ii:128 * ii + 128]

    operate(0, emit_out)
    wait_plane(3, lambda other: ib_g.at[other])

    @pl.loop(0, 8)
    def _(m):
        for ii, tile in enumerate(merged(ib_g, m)):
            here = lanes(m, ii)
            out_ref[:, here] = out_ref[:, here] + tile

    by_color(spread_sent)
    energy_copy.wait_send()
    pair_copy(0, fsib, fr).wait_send()
    pair_copy(1, psib, pr).wait_send()
    sent_plane(0, lambda other: rows24(grid_v, other))
    sent_plane(1, lambda other: rows24(grid_t, other))
    sent_plane(2, lambda other: ib_f.at[other])
    sent_plane(3, lambda other: ib_g.at[other])
    for kind, ref in enumerate((sent_v, sent_t, sent_f, sent_g)):
        sent_z(kind, ref)


def shards(coeffs, diagonal, shift, rotation, string_blocks, block_cols):
    vmem = pl.BlockSpec(memory_space=pltpu.VMEM)
    smem = pl.BlockSpec(memory_space=pltpu.SMEM)
    hbm = pl.BlockSpec(memory_space=pltpu.HBM)
    rows = pltpu.VMEM((24, 3072), F32)
    grid = pltpu.VMEM((384, 256), F32)
    packed = pltpu.VMEM((16, 36, 128), F32)
    coded = pltpu.VMEM((16, 40, 128), jnp.int16)
    chunks = pltpu.VMEM((24, 24, 128), F32)
    windows = pltpu.VMEM((16, 24, 256), F32)
    wide = pltpu.VMEM((8, 24, 384), F32)
    dma = pltpu.SemaphoreType.DMA
    result = pl.pallas_call(
        kernel,
        out_shape=jax.ShapeDtypeStruct((24, 3072), F32),
        in_specs=[hbm, hbm, smem, smem, hbm, smem],
        out_specs=vmem,
        scratch_shapes=[
            rows, rows, pltpu.VMEM((8, 4, 4, 240, 128), BF16),
            grid, grid, pltpu.VMEM((256, 128), F32),
            packed, packed, packed, packed, packed, packed, packed, packed,
            coded, coded, coded, coded, coded, coded, coded, coded,
            pltpu.VMEM((24, 48, 128), BF16),
            chunks, chunks, wide,
            chunks, chunks, chunks, chunks, chunks, chunks,
            grid, grid, windows, windows, wide,
            pltpu.VMEM((2, 8, 128), F32),
            dma((len(PLAN),)), dma((len(PLAN),)), dma((3,)),
            dma((5, 16)), dma((5, 16)), dma((4, 16)), dma((4, 16)), dma((3,)), dma((3,)),
        ],
        compiler_params=pltpu.CompilerParams(
            collective_id=0, has_side_effects=True, vmem_limit_bytes=67043328),
        name="filter",
    )(coeffs, diagonal, shift, rotation, string_blocks, block_cols.T)
    return result[None]


def solution(mesh):
    split_mesh = Mesh(mesh.devices.reshape(2, 2, 8, 4, 4), ROOT + COL)
    return jax.shard_map(
        shards,
        mesh=split_mesh,
        in_specs=(P(ROOT, COL, None), P(COL, None), P(ROOT), P(), P(COL, None), P()),
        out_specs=P(ROOT, COL, None),
        check_vma=False,
    )
```

```python
import jax
import jax.numpy as jnp
from jax import lax
from jax.experimental import pallas as pl
from jax.experimental.pallas import tpu as pltpu
from jax.sharding import Mesh
from jax.sharding import PartitionSpec as P

ROOT = ("zh", "core")
COL = ("zl", "y", "x")
CUT = 128
PARTS = (((0, 96), (96, 32)), ((CUT, 80), (CUT + 80, 32)))
F32, BF16 = jnp.float32, jnp.bfloat16
ONTO = pl.DeviceIdType.MESH

E, H, Q = (0, 8), ((0, 4), (4, 4)), ((0, 2), (2, 2), (4, 2), (6, 2))
Z_STEPS = (1, -1, 2, -2, 3, -3, 4)


def spread_plan():
    plan = [("z", ("z", d), None) for d in Z_STEPS]

    def both(zs, a):
        plan.append(((zs, a, 0), ("second", 1), (zs, a, -1)))
        plan.append(((zs, a, 0), ("second", -1), (zs, a, 1)))

    def sibling(zs, a, b):
        plan.append(((zs, a, b), ("core", 1), "sibling"))

    plan.append(((E, 0, 0), ("first", 1), (E, -1, 0)))
    plan.append(((E, 0, 0), ("first", -1), (E, 1, 0)))
    both(E, 0)
    sibling(E, 0, 0)
    marks = {"start": (7, 12)}
    steps = []
    n = len(plan)
    plan.append(((H[0], -1, 0), ("first", 1), (H[0], -2, 0)))
    both(E, -1)
    sibling(E, -1, 0)
    steps.append((7, (n, len(plan))))
    far_low = n
    n = len(plan)
    plan.append(((H[1], 1, 0), ("first", -1), (H[1], 2, 0)))
    both(E, 1)
    sibling(E, 1, 0)
    steps.append((8, (n, len(plan))))
    far_high = n
    n = len(plan)
    both(H[0], 2)
    sibling(H[0], 2, 0)
    steps.append((far_low, (n, len(plan))))
    n = len(plan)
    both(H[1], 2)
    sibling(H[1], 2, 0)
    steps.append((far_high, (n, len(plan))))
    sets = [(0, E, H[0], H[1], 9), (-1, E, H[0], H[1], 13), (1, E, H[0], H[1], 17),
            (2, H[0], Q[0], Q[1], 20), (2, H[1], Q[2], Q[3], 23)]
    last = []
    for a, zs, low, high, number in sets:
        n = len(plan)
        plan.append(((low, a, -1), ("second", 1), (low, a, -2)))
        sibling(zs, a, -1)
        steps.append((number, (n, len(plan))))
        last.append((n, low, a))
        n = len(plan)
        plan.append(((high, a, 1), ("second", -1), (high, a, 2)))
        sibling(zs, a, 1)
        steps.append((number + 1, (n, len(plan))))
        last.append((n, high, a))
    lasts = []
    for number, zs, a in last:
        n = len(plan)
        sibling(zs, a, 2)
        lasts.append((number, (n, len(plan))))

    def ring(part, half, way):
        plan.append((("ring", part, half), ("z", way), ("ring", part - way, half)))
        return len(plan) - 1

    def ring_sibling(part, half=None):
        plan.append((("ring", part, half), ("core", 1), "sibling"))

    n = len(plan)
    up, down = ring(0, None, 1), ring(0, None, -1)
    ring_sibling(0)
    marks["ring"] = (n, len(plan))
    rings = []
    for hop in (1, 2, 3):
        n = len(plan)
        next_up = ring(-hop, 0 if hop == 3 else None, 1)
        ring_sibling(-hop)
        rings.append((up, (n, len(plan))))
        n = len(plan)
        next_down = ring(hop, 1 if hop == 3 else None, -1)
        ring_sibling(hop)
        rings.append((down, (n, len(plan))))
        up, down = next_up, next_down
    for number, part, half in ((up, -4, 0), (down, 4, 1)):
        n = len(plan)
        ring_sibling(part, half)
        rings.append((number, (n, len(plan))))
    early = steps[0:2] + rings[0:2] + steps[2:8] + rings[2:4] + steps[8:12] + rings[4:6]
    late = steps[12:] + lasts + rings[6:8]
    return plan, marks, early, late


PLAN, MARKS, EARLY, LATE = spread_plan()


def device(z, y, x, core):
    return {"zh": z // 8, "core": core, "zl": lax.rem(z, 8), "y": y, "x": x}


def split(value):
    high = value.astype(BF16).astype(F32)
    return jnp.concatenate([high, value - high], axis=0).astype(BF16)


def kernel(v_any, diag_any, shift_ref, rot_ref, mine_ref, cols_ref, out_ref,
           v_ref, diag_ref, op, grid_v, grid_t, turn, zs_v, zs_t, zs_f, zs_g, zb_v, zb_t, zb_f, zb_g,
           sent_v, sent_t, sent_f, sent_g, got_v, got_t, got_f, got_g,
           xb, vc, rv, tb, fm, fsib, pm, psib, fr, pr, wf, wg, ib_f, ib_g, hf, eb,
           op_send, op_recv, local, plane_send, plane_recv, z_send, z_recv, pair_send, pair_recv, vouch):
    zh, core, zl = lax.axis_index("zh"), lax.axis_index("core"), lax.axis_index("zl")
    y, x = lax.axis_index("y"), lax.axis_index("x")
    z = zh * 8 + zl
    p = y * 4 + x

    def at_z(other):
        return device(other, y, x, core)

    def at_p(other):
        return {"zh": zh, "core": core, "zl": zl, "y": other // 4, "x": lax.rem(other, 4)}

    pair = {"zh": zh, "core": 1 - core, "zl": zl, "y": y, "x": x}

    barrier = pltpu.get_barrier_semaphore()

    @pl.loop(1, 16)
    def _(step):
        pl.semaphore_signal(barrier, inc=1, device_id=at_p(lax.rem(p + step, 16)), device_id_type=ONTO)

    for step in (4, -4, 3, -3, 2, -2, 1, -1):
        pl.semaphore_signal(barrier, inc=1, device_id=at_z(lax.rem(z + step + 16, 16)), device_id_type=ONTO)

    pl.semaphore_signal(barrier, inc=1, device_id=pair, device_id_type=ONTO)
    load_v = pltpu.make_async_copy(v_any.at[0], v_ref, local.at[0])
    load_diag = pltpu.make_async_copy(diag_any, diag_ref, local.at[1])
    load_v.start()
    load_diag.start()

    @pl.when(core == 0)
    def _():
        part = pl.ds(0, CUT)
        load = pltpu.make_async_copy(mine_ref.at[part], op.at[zl, y, x, part], local.at[2])
        load.start()
        load.wait()

    @pl.when(core == 1)
    def _():
        part = pl.ds(CUT, 240 - CUT)
        load = pltpu.make_async_copy(mine_ref.at[part], op.at[zl, y, x, part], local.at[2])
        load.start()
        load.wait()

    energy = shift_ref[0]
    eb[zh] = jnp.full((8, 128), energy, F32)
    turn[...] = jnp.zeros_like(turn)
    load_v.wait()
    load_diag.wait()
    grid_v[pl.ds(pl.multiple_of(p * 24, 8), 24), :] = v_ref[
        :, pl.ds(pl.multiple_of((3 * (p // 2) + lax.rem(p, 2)) * 128, 128), 256)]

    @pl.loop(0, 24)
    def _(c):
        xb[c] = split(v_ref[:, pl.ds(pl.multiple_of(c * 128, 128), 128)])

    pl.semaphore_wait(barrier, 24)
    for step in (4, -4):
        pl.semaphore_signal(vouch, inc=1, device_id=at_z(lax.rem(z + step + 16, 16)), device_id_type=ONTO)

    def plane_copy(kind, src, dst, to, source):
        return pltpu.make_async_remote_copy(
            src_ref=src, dst_ref=dst, send_sem=plane_send.at[kind, to], recv_sem=plane_recv.at[kind, source],
            device_id=at_p(to), device_id_type=ONTO)

    def z_copy(kind, src, dst, to, source):
        return pltpu.make_async_remote_copy(
            src_ref=src, dst_ref=dst, send_sem=z_send.at[kind, to], recv_sem=z_recv.at[kind, source],
            device_id=at_z(to), device_id_type=ONTO)

    def rows24(ref, index):
        return ref.at[pl.ds(pl.multiple_of(index * 24, 8), 24), :]

    def wait_plane(kind, slot):
        @pl.loop(1, 16)
        def _(step):
            other = lax.rem(p + step, 16)
            plane_copy(kind, slot(other), slot(other), other, other).wait_recv()

    def wait_z(kind, ref):
        @pl.loop(1, 16)
        def _(step):
            other = lax.rem(z + step, 16)
            z_copy(kind, ref.at[other], ref.at[other], other, other).wait_recv()

    def sent_plane(kind, slot):
        @pl.loop(1, 16)
        def _(step):
            other = lax.rem(p + step, 16)
            plane_copy(kind, slot(other), slot(other), other, other).wait_send()

    def sent_z(kind, ref):
        @pl.loop(1, 16)
        def _(step):
            other = lax.rem(z + step, 16)
            z_copy(kind, ref.at[other], ref.at[other], other, other).wait_send()

    def spread(color):
        rows, around = PARTS[color]
        others, others_around = PARTS[1 - color]
        place = {"y": y, "x": x}

        def of(piece, part, first, second):
            zs, a, b = piece
            if zs == "ring":
                which = pl.ds(0, 4) if b is None else pl.ds(2 * b, 2)
                return op.at[lax.rem(zl + a + 8, 8), which, :, pl.ds(part[0], part[1])]
            index = {first: lax.rem(place[first] + a + 4, 4), second: lax.rem(place[second] + b + 4, 4)}
            return op.at[pl.ds(zs[0], zs[1]), index["y"], index["x"], pl.ds(part[0], part[1])]

        first, second = ("y", "x") if color == 0 else ("x", "y")

        def copy(number, landing=False):
            piece, (axis, step), lands = PLAN[number]
            if piece == "z":
                source = lax.rem(zl - step + 8, 8) if landing else zl
                ref = op.at[source, y, x, pl.ds(rows[0], rows[1])]
                to = at_z(lax.rem(z + step + 16, 16))
            elif axis == "core":
                going = around if piece[0] == "ring" else rows
                coming = others_around if piece[0] == "ring" else others
                ref = of(piece, coming, second, first) if landing else of(piece, going, first, second)
                to = pair
            elif axis == "z":
                ref = of(lands if landing else piece, around, first, second)
                to = at_z(lax.rem(z + step + 16, 16))
            else:
                ref = of(lands if landing else piece, rows, first, second)
                name = first if axis == "first" else second
                there = dict(place)
                there[name] = lax.rem(place[name] + step + 4, 4)
                to = device(z, there["y"], there["x"], core)
            return pltpu.make_async_remote_copy(
                src_ref=ref, dst_ref=ref, send_sem=op_send.at[number], recv_sem=op_recv.at[number],
                device_id=to, device_id_type=ONTO)

        return around, copy

    def by_color(body):
        for color in (0, 1):
            @pl.when(core == color)
            def _():
                body(*spread(color))

    def spread_start(around, copy):
        for number in range(7):
            copy(number).start()

        @pl.loop(1, 16)
        def _(step):
            target = lax.rem(p + step, 16)
            around_copy(around, p, target, p).start()

    def around_copy(around, source_slot, to, source):
        ref = op.at[zl, source_slot // 4, lax.rem(source_slot, 4), pl.ds(around[0], around[1])]
        return plane_copy(4, ref, ref, to, source)

    def spread_on(around, copy):
        for number in range(7):
            copy(number, True).wait_recv()
        for number in range(*MARKS["start"]):
            copy(number).start()

        @pl.loop(1, 16)
        def _(step):
            other = lax.rem(p + step, 16)
            around_copy(around, other, other, other).wait_recv()

        for number in range(*MARKS["ring"]):
            copy(number).start()
        follow_on(EARLY[:4], copy)

    def follow_on(steps, copy):
        for number, (low, high) in steps:
            copy(number, True).wait_recv()
            for follow in range(low, high):
                copy(follow).start()

    def spread_rest(around, copy):
        follow_on(EARLY[4:] + LATE, copy)
        for number in range(len(PLAN)):
            if PLAN[number][1][0] == "core":
                copy(number, True).wait_recv()

    def spread_sent(around, copy):
        for number in range(len(PLAN)):
            copy(number).wait_send()

        @pl.loop(1, 16)
        def _(step):
            other = lax.rem(p + step, 16)
            around_copy(around, p, other, other).wait_send()

    def window(target):
        return pl.ds(pl.multiple_of((3 * (target // 2) + lax.rem(target, 2)) * 128, 128), 256)

    half = pl.ds(pl.multiple_of(lax.rem(p, 2) * 64, 64), 192)
    mine24 = pl.ds(pl.multiple_of(p * 24, 8), 24)

    def turn_rows(grid, zs):
        for k in range(3):
            rows = slice(128 * k, 128 * k + 128)
            turn[0:128, :] = grid[rows, 0:128].T
            turn[128:256, :] = grid[rows, 128:256].T
            columns = turn[half, :]
            for target in range(16):
                zs[target, 12 * k:12 * k + 12, :] = columns[12 * target:12 * target + 12]

    own_lane = lax.broadcasted_iota(jnp.int32, (36, 128), 0) == lax.broadcasted_iota(jnp.int32, (36, 128), 1)

    def encode(zs, codes, target):
        value = zs[target]
        top = jnp.maximum(jnp.max(jnp.abs(value), axis=1, keepdims=True), 1e-30)
        level = jnp.ceil(jnp.log2(top) * 128.0)
        scaled = jnp.round(value * (jnp.exp2(level * (-1.0 / 128.0)) * 32700.0))
        levels = jnp.sum(jnp.where(own_lane, level, 0.0), axis=0, keepdims=True)
        whole = jnp.concatenate([scaled, jnp.broadcast_to(levels, (4, 128))], axis=0)
        codes[target] = whole.astype(jnp.int32).astype(jnp.int16)

    def decode(codes, zb):
        @pl.loop(0, 4)
        def _(quarter):
            for one in range(4):
                source = quarter * 4 + one
                whole = codes[source].astype(jnp.int32).astype(F32)
                levels = jnp.broadcast_to(whole[36:37], (36, 128))
                level = jnp.sum(jnp.where(own_lane, levels, 0.0), axis=1, keepdims=True)
                zb[source] = whole[0:36] * (jnp.exp2(level * (1.0 / 128.0)) * (1.0 / 32700.0))

    def send_z(kind, zs, zb, target):
        @pl.when(target != z)
        def _():
            z_copy(kind, zs.at[target], zb.at[z], target, z).start()

        @pl.when(target == z)
        def _():
            zb[z] = zs[z]

    def send_all_z(kind, zs, codes, landing):
        @pl.loop(0, 4)
        def _(step):
            group = [lax.rem(z + 16 + way, 16) for way in
                     (2 * step - 8, 7 - 2 * step, 2 * step - 7, 6 - 2 * step)]
            for target in group:
                encode(zs, codes, target)
            for target in group:
                send_z(kind, codes, landing, target)

    def turn_columns(zb, rows_out):
        for k in range(3):
            turn[half, :] = jnp.concatenate([zb[source, 12 * k:12 * k + 12, :] for source in range(16)], axis=0)
            rows = slice(128 * k, 128 * k + 128)
            rows_out[rows, 0:128] = turn[0:128, :].T
            rows_out[rows, 128:256] = turn[128:256, :].T

    def send_rows(kind, rows_out, ib):
        @pl.loop(1, 16)
        def _(step):
            target = lax.rem(p + step, 16)
            plane_copy(kind, rows24(rows_out, target), ib.at[p], target, p).start()

        ib[p] = rows_out[mine24, :]

    low_lanes = lax.broadcasted_iota(jnp.int32, (24, 128), 1) < 64

    def merged(ib, m):
        even, odd = ib[2 * m], ib[2 * m + 1]
        return even[:, 0:128], jnp.where(low_lanes, even[:, 128:256], odd[:, 0:128]), odd[:, 128:256]

    def block(m, ii, f):
        row = ii * 1280 + f * 128
        parts, left = [], 128
        while left:
            place, offset = divmod(row, 240)
            take = min(left, 240 - offset)
            parts.append(op[m, place // 4, place % 4, offset:offset + take, :])
            row, left = row + take, left - take
        return parts[0] if len(parts) == 1 else jnp.concatenate(parts, axis=0)

    def outward(step):
        return jnp.where(lax.rem(step, 2) == 1, (step + 1) // 2, 8 - step // 2)

    def operate(first, emit, after=None, order=lambda step: step):
        @pl.loop(0, 8)
        def _(step):
            m = lax.rem(first + order(step), 8)
            for ii in range(3):
                vectors = jnp.concatenate([xb[cols_ref[f, 3 * m + ii]] for f in range(10)], axis=1)
                blocks = jnp.concatenate([block(m, ii, f) for f in range(10)], axis=1)
                both = lax.dot_general(vectors, blocks, (((1,), (1,)), ((), ())), preferred_element_type=F32)
                emit(m, ii, both[0:24] + both[24:48])
            if after is not None:
                after(m)

    def lanes(m, ii):
        return pl.ds(pl.multiple_of((3 * m + ii) * 128, 128), 128)

    by_color(spread_start)

    @pl.loop(1, 16)
    def _(step):
        target = lax.rem(p + step, 16)
        plane_copy(0, v_ref.at[:, window(target)], grid_v.at[mine24, :], target, p).start()


    by_color(spread_on)
    pl.semaphore_wait(vouch, 2)
    energy_copy = pltpu.make_async_remote_copy(
        src_ref=eb.at[zh], dst_ref=eb.at[zh], send_sem=pair_send.at[2], recv_sem=pair_recv.at[2],
        device_id=at_z(lax.rem(z + 8, 16)), device_id_type=ONTO)
    energy_copy.start()
    wait_plane(0, lambda other: rows24(grid_v, other))
    turn_rows(grid_v, zs_v)
    send_all_z(0, zs_v, sent_v, got_v)
    by_color(spread_rest)

    def emit_t(m, ii, value):
        here = lanes(m, ii)
        tb[m, :, 128 * ii:128 * ii + 128] = value + (diag_ref[:, here] - energy) * v_ref[:, here]

    def after_t(m):
        for odd in (0, 1):
            target = 2 * m + odd
            part = tb.at[m, :, pl.ds(128 * odd, 256)]

            @pl.when(target != p)
            def _():
                plane_copy(1, part, grid_t.at[mine24, :], target, p).start()

            @pl.when(target == p)
            def _():
                grid_t[mine24, :] = tb[m, :, 128 * odd:128 * odd + 256]

    operate(lax.rem(p // 2 + 1, 8), emit_t, after_t)

    wait_plane(1, lambda other: rows24(grid_t, other))
    turn_rows(grid_t, zs_t)
    send_all_z(1, zs_t, sent_t, got_t)

    wait_z(0, got_v)
    decode(got_v, zb_v)

    @pl.loop(0, 8)
    def _(m):
        for k in range(3):
            part = slice(12 * k, 12 * k + 12)
            both = jnp.concatenate([zb_v[m, part, :], zb_v[8 + m, part, :]], axis=0)
            vc[3 * m + k] = both
            xb[3 * m + k] = split(both)

    def emit_rv(m, ii, value):
        rv[3 * m + ii] = value

    operate(0, emit_rv)
    wait_z(1, got_t)
    decode(got_t, zb_t)

    other_energy = pltpu.make_async_remote_copy(
        src_ref=eb.at[1 - zh], dst_ref=eb.at[1 - zh], send_sem=pair_send.at[2], recv_sem=pair_recv.at[2],
        device_id=at_z(lax.rem(z + 8, 16)), device_id_type=ONTO)
    other_energy.wait_recv()
    upper = lax.broadcasted_iota(jnp.int32, (24, 128), 0) < 12
    shifts = jnp.where(upper, jnp.broadcast_to(eb[0, 0:1, :], (24, 128)), jnp.broadcast_to(eb[1, 0:1, :], (24, 128)))

    def weights(to_core):
        straight = jnp.where(upper, rot_ref[to_core, core], rot_ref[2 + to_core, 2 + core])
        crossed = jnp.where(upper, rot_ref[to_core, 2 + core], rot_ref[2 + to_core, core])
        return straight, crossed

    here_straight, here_crossed = weights(core)
    there_straight, there_crossed = weights(1 - core)

    def swapped(value):
        return jnp.concatenate([value[12:24], value[0:12]], axis=0)

    def pair_copy(index, src, dst):
        return pltpu.make_async_remote_copy(
            src_ref=src, dst_ref=dst, send_sem=pair_send.at[index], recv_sem=pair_recv.at[index],
            device_id=pair, device_id_type=ONTO)

    @pl.loop(0, 8)
    def _(m):
        for k in range(3):
            c = 3 * m + k
            part = slice(12 * k, 12 * k + 12)
            t = jnp.concatenate([zb_t[m, part, :], zb_t[8 + m, part, :]], axis=0)
            first = 0.5 * (rv[c] + t)
            turned = swapped(first)
            rv[c] = first
            fm[c] = here_straight * first + here_crossed * turned
            fsib[c] = there_straight * first + there_crossed * turned

    pair_copy(0, fsib, fr).start()

    @pl.loop(0, 8)
    def _(m):
        for k in range(3):
            c = 3 * m + k
            rest = shifts * rv[c] + vc[c]
            rest_turned = swapped(rest)
            pm[c] = here_straight * rest + here_crossed * rest_turned
            psib[c] = there_straight * rest + there_crossed * rest_turned

    pair_copy(1, psib, pr).start()
    pair_copy(0, fsib, fr).wait_recv()

    @pl.loop(0, 8)
    def _(step):
        m = lax.rem(zl + outward(step), 8)
        for k in range(3):
            c = 3 * m + k
            value = fm[c] + fr[c]
            xb[c] = split(value)
            zs_f[m, 12 * k:12 * k + 12, :] = value[0:12]
            zs_f[8 + m, 12 * k:12 * k + 12, :] = value[12:24]
        encode(zs_f, sent_f, m)
        encode(zs_f, sent_f, m + 8)
        send_z(2, sent_f, got_f, m)
        send_z(2, sent_f, got_f, m + 8)

    pair_copy(1, psib, pr).wait_recv()

    def emit_g(m, ii, value):
        c = 3 * m + ii
        g = value - (pm[c] + pr[c])
        zs_g[m, 12 * ii:12 * ii + 12, :] = g[0:12]
        zs_g[8 + m, 12 * ii:12 * ii + 12, :] = g[12:24]

    def after_g(m):
        encode(zs_g, sent_g, m)
        encode(zs_g, sent_g, m + 8)
        send_z(3, sent_g, got_g, m)
        send_z(3, sent_g, got_g, m + 8)

    operate(zl, emit_g, after_g, outward)

    wait_z(2, got_f)
    decode(got_f, zb_f)
    turn_columns(zb_f, wf)
    send_rows(2, wf, ib_f)
    wait_z(3, got_g)
    decode(got_g, zb_g)
    turn_columns(zb_g, wg)
    send_rows(3, wg, ib_g)
    wait_plane(2, lambda other: ib_f.at[other])

    @pl.loop(0, 8)
    def _(m):
        for ii, tile in enumerate(merged(ib_f, m)):
            hf[m, :, 128 * ii:128 * ii + 128] = tile
            xb[3 * m + ii] = split(tile)

    def emit_out(m, ii, value):
        here = lanes(m, ii)
        out_ref[:, here] = value + diag_ref[:, here] * hf[m, :, 128 * ii:128 * ii + 128]

    operate(0, emit_out)
    wait_plane(3, lambda other: ib_g.at[other])

    @pl.loop(0, 8)
    def _(m):
        for ii, tile in enumerate(merged(ib_g, m)):
            here = lanes(m, ii)
            out_ref[:, here] = out_ref[:, here] + tile

    by_color(spread_sent)
    energy_copy.wait_send()
    pair_copy(0, fsib, fr).wait_send()
    pair_copy(1, psib, pr).wait_send()
    sent_plane(0, lambda other: rows24(grid_v, other))
    sent_plane(1, lambda other: rows24(grid_t, other))
    sent_plane(2, lambda other: ib_f.at[other])
    sent_plane(3, lambda other: ib_g.at[other])
    for kind, ref in enumerate((sent_v, sent_t, sent_f, sent_g)):
        sent_z(kind, ref)


def shards(coeffs, diagonal, shift, rotation, string_blocks, block_cols):
    vmem = pl.BlockSpec(memory_space=pltpu.VMEM)
    smem = pl.BlockSpec(memory_space=pltpu.SMEM)
    hbm = pl.BlockSpec(memory_space=pltpu.HBM)
    rows = pltpu.VMEM((24, 3072), F32)
    grid = pltpu.VMEM((384, 256), F32)
    packed = pltpu.VMEM((16, 36, 128), F32)
    coded = pltpu.VMEM((16, 40, 128), jnp.int16)
    chunks = pltpu.VMEM((24, 24, 128), F32)
    windows = pltpu.VMEM((16, 24, 256), F32)
    wide = pltpu.VMEM((8, 24, 384), F32)
    dma = pltpu.SemaphoreType.DMA
    result = pl.pallas_call(
        kernel,
        out_shape=jax.ShapeDtypeStruct((24, 3072), F32),
        in_specs=[hbm, hbm, smem, smem, hbm, smem],
        out_specs=vmem,
        scratch_shapes=[
            rows, rows, pltpu.VMEM((8, 4, 4, 240, 128), BF16),
            grid, grid, pltpu.VMEM((256, 128), F32),
            packed, packed, packed, packed, packed, packed, packed, packed,
            coded, coded, coded, coded, coded, coded, coded, coded,
            pltpu.VMEM((24, 48, 128), BF16),
            chunks, chunks, wide,
            chunks, chunks, chunks, chunks, chunks, chunks,
            grid, grid, windows, windows, wide,
            pltpu.VMEM((2, 8, 128), F32),
            dma((len(PLAN),)), dma((len(PLAN),)), dma((3,)),
            dma((5, 16)), dma((5, 16)), dma((4, 16)), dma((4, 16)), dma((3,)), dma((3,)),
            pltpu.SemaphoreType.REGULAR,
        ],
        compiler_params=pltpu.CompilerParams(
            collective_id=0, has_side_effects=True, vmem_limit_bytes=67043328),
        name="filter",
    )(coeffs, diagonal, shift, rotation, string_blocks, block_cols.T)
    return result[None]


def solution(mesh):
    split_mesh = Mesh(mesh.devices.reshape(2, 2, 8, 4, 4), ROOT + COL)
    return jax.shard_map(
        shards,
        mesh=split_mesh,
        in_specs=(P(ROOT, COL, None), P(COL, None), P(ROOT), P(), P(COL, None), P()),
        out_specs=P(ROOT, COL, None),
        check_vma=False,
    )
```

```python
import jax
import jax.numpy as jnp
from jax import lax
from jax.experimental import pallas as pl
from jax.experimental.pallas import tpu as pltpu
from jax.sharding import Mesh
from jax.sharding import PartitionSpec as P

ROOT = ("zh", "core")
COL = ("zl", "y", "x")
CUT = 128
PARTS = (((0, 96), (96, 32)), ((CUT, 80), (CUT + 80, 32)))
F32, BF16 = jnp.float32, jnp.bfloat16
ONTO = pl.DeviceIdType.MESH

E, H, Q = (0, 8), ((0, 4), (4, 4)), ((0, 2), (2, 2), (4, 2), (6, 2))
Z_STEPS = (1, -1, 2, -2, 3, -3, 4)


def spread_plan():
    plan = [("z", ("z", d), None) for d in Z_STEPS]

    def both(zs, a):
        plan.append(((zs, a, 0), ("second", 1), (zs, a, -1)))
        plan.append(((zs, a, 0), ("second", -1), (zs, a, 1)))

    def sibling(zs, a, b):
        plan.append(((zs, a, b), ("core", 1), "sibling"))

    plan.append(((E, 0, 0), ("first", 1), (E, -1, 0)))
    plan.append(((E, 0, 0), ("first", -1), (E, 1, 0)))
    both(E, 0)
    sibling(E, 0, 0)
    marks = {"start": (7, 12)}
    steps = []
    n = len(plan)
    plan.append(((H[0], -1, 0), ("first", 1), (H[0], -2, 0)))
    both(E, -1)
    sibling(E, -1, 0)
    steps.append((7, (n, len(plan))))
    far_low = n
    n = len(plan)
    plan.append(((H[1], 1, 0), ("first", -1), (H[1], 2, 0)))
    both(E, 1)
    sibling(E, 1, 0)
    steps.append((8, (n, len(plan))))
    far_high = n
    n = len(plan)
    both(H[0], 2)
    sibling(H[0], 2, 0)
    steps.append((far_low, (n, len(plan))))
    n = len(plan)
    both(H[1], 2)
    sibling(H[1], 2, 0)
    steps.append((far_high, (n, len(plan))))
    sets = [(0, E, H[0], H[1], 9), (-1, E, H[0], H[1], 13), (1, E, H[0], H[1], 17),
            (2, H[0], Q[0], Q[1], 20), (2, H[1], Q[2], Q[3], 23)]
    last = []
    for a, zs, low, high, number in sets:
        n = len(plan)
        plan.append(((low, a, -1), ("second", 1), (low, a, -2)))
        sibling(zs, a, -1)
        steps.append((number, (n, len(plan))))
        last.append((n, low, a))
        n = len(plan)
        plan.append(((high, a, 1), ("second", -1), (high, a, 2)))
        sibling(zs, a, 1)
        steps.append((number + 1, (n, len(plan))))
        last.append((n, high, a))
    lasts = []
    for number, zs, a in last:
        n = len(plan)
        sibling(zs, a, 2)
        lasts.append((number, (n, len(plan))))

    def ring(part, half, way):
        plan.append((("ring", part, half), ("z", way), ("ring", part - way, half)))
        return len(plan) - 1

    def ring_sibling(part, half=None):
        plan.append((("ring", part, half), ("core", 1), "sibling"))

    n = len(plan)
    up, down = ring(0, None, 1), ring(0, None, -1)
    ring_sibling(0)
    marks["ring"] = (n, len(plan))
    rings = []
    for hop in (1, 2, 3):
        n = len(plan)
        next_up = ring(-hop, 0 if hop == 3 else None, 1)
        ring_sibling(-hop)
        rings.append((up, (n, len(plan))))
        n = len(plan)
        next_down = ring(hop, 1 if hop == 3 else None, -1)
        ring_sibling(hop)
        rings.append((down, (n, len(plan))))
        up, down = next_up, next_down
    for number, part, half in ((up, -4, 0), (down, 4, 1)):
        n = len(plan)
        ring_sibling(part, half)
        rings.append((number, (n, len(plan))))
    early = steps[0:2] + rings[0:2] + steps[2:8] + rings[2:4] + steps[8:12] + rings[4:6]
    late = steps[12:] + lasts + rings[6:8]
    return plan, marks, early, late


PLAN, MARKS, EARLY, LATE = spread_plan()


def device(z, y, x, core):
    return {"zh": z // 8, "core": core, "zl": lax.rem(z, 8), "y": y, "x": x}


def split(value):
    high = value.astype(BF16).astype(F32)
    return jnp.concatenate([high, value - high], axis=0).astype(BF16)


def kernel(v_any, diag_any, shift_ref, rot_ref, mine_ref, cols_ref, out_ref,
           v_ref, diag_ref, op, grid_v, grid_t, turn, zs_v, zs_t, zs_f, zs_g, zb_v, zb_t, zb_f, zb_g,
           sent_v, sent_t, sent_f, sent_g, got_v, got_t, got_f, got_g,
           xb, vc, rv, tb, fm, fsib, pm, psib, fr, pr, wf, wg, ib_f, ib_g, hf, eb,
           op_send, op_recv, local, plane_send, plane_recv, z_send, z_recv, pair_send, pair_recv, vouch):
    zh, core, zl = lax.axis_index("zh"), lax.axis_index("core"), lax.axis_index("zl")
    y, x = lax.axis_index("y"), lax.axis_index("x")
    z = zh * 8 + zl
    p = y * 4 + x

    def at_z(other):
        return device(other, y, x, core)

    def at_p(other):
        return {"zh": zh, "core": core, "zl": zl, "y": other // 4, "x": lax.rem(other, 4)}

    pair = {"zh": zh, "core": 1 - core, "zl": zl, "y": y, "x": x}

    barrier = pltpu.get_barrier_semaphore()

    @pl.loop(1, 16)
    def _(step):
        pl.semaphore_signal(barrier, inc=1, device_id=at_p(lax.rem(p + step, 16)), device_id_type=ONTO)

    for step in (4, -4, 3, -3, 2, -2, 1, -1):
        pl.semaphore_signal(barrier, inc=1, device_id=at_z(lax.rem(z + step + 16, 16)), device_id_type=ONTO)

    pl.semaphore_signal(barrier, inc=1, device_id=pair, device_id_type=ONTO)
    load_v = pltpu.make_async_copy(v_any.at[0], v_ref, local.at[0])
    load_diag = pltpu.make_async_copy(diag_any, diag_ref, local.at[1])
    @pl.when(core == 0)
    def _():
        part = pl.ds(0, CUT)
        load = pltpu.make_async_copy(mine_ref.at[part], op.at[zl, y, x, part], local.at[2])
        load.start()
        load_v.start()
        load_diag.start()
        load.wait()

    @pl.when(core == 1)
    def _():
        part = pl.ds(CUT, 240 - CUT)
        load = pltpu.make_async_copy(mine_ref.at[part], op.at[zl, y, x, part], local.at[2])
        load.start()
        load_v.start()
        load_diag.start()
        load.wait()

    pl.semaphore_wait(barrier, 24)
    for step in (4, -4):
        pl.semaphore_signal(vouch, inc=1, device_id=at_z(lax.rem(z + step + 16, 16)), device_id_type=ONTO)

    def plane_copy(kind, src, dst, to, source):
        return pltpu.make_async_remote_copy(
            src_ref=src, dst_ref=dst, send_sem=plane_send.at[kind, to], recv_sem=plane_recv.at[kind, source],
            device_id=at_p(to), device_id_type=ONTO)

    def z_copy(kind, src, dst, to, source):
        return pltpu.make_async_remote_copy(
            src_ref=src, dst_ref=dst, send_sem=z_send.at[kind, to], recv_sem=z_recv.at[kind, source],
            device_id=at_z(to), device_id_type=ONTO)

    def rows24(ref, index):
        return ref.at[pl.ds(pl.multiple_of(index * 24, 8), 24), :]

    def wait_plane(kind, slot):
        @pl.loop(1, 16)
        def _(step):
            other = lax.rem(p + step, 16)
            plane_copy(kind, slot(other), slot(other), other, other).wait_recv()

    def sent_plane(kind, slot):
        @pl.loop(1, 16)
        def _(step):
            other = lax.rem(p + step, 16)
            plane_copy(kind, slot(other), slot(other), other, other).wait_send()

    def sent_z(kind, ref):
        @pl.loop(1, 16)
        def _(step):
            other = lax.rem(z + step, 16)
            z_copy(kind, ref.at[other], ref.at[other], other, other).wait_send()

    def spread(color):
        rows, around = PARTS[color]
        others, others_around = PARTS[1 - color]
        place = {"y": y, "x": x}

        def of(piece, part, first, second):
            zs, a, b = piece
            if zs == "ring":
                which = pl.ds(0, 4) if b is None else pl.ds(2 * b, 2)
                return op.at[lax.rem(zl + a + 8, 8), which, :, pl.ds(part[0], part[1])]
            index = {first: lax.rem(place[first] + a + 4, 4), second: lax.rem(place[second] + b + 4, 4)}
            return op.at[pl.ds(zs[0], zs[1]), index["y"], index["x"], pl.ds(part[0], part[1])]

        first, second = ("y", "x") if color == 0 else ("x", "y")

        def copy(number, landing=False):
            piece, (axis, step), lands = PLAN[number]
            if piece == "z":
                source = lax.rem(zl - step + 8, 8) if landing else zl
                ref = op.at[source, y, x, pl.ds(rows[0], rows[1])]
                to = at_z(lax.rem(z + step + 16, 16))
            elif axis == "core":
                going = around if piece[0] == "ring" else rows
                coming = others_around if piece[0] == "ring" else others
                ref = of(piece, coming, second, first) if landing else of(piece, going, first, second)
                to = pair
            elif axis == "z":
                ref = of(lands if landing else piece, around, first, second)
                to = at_z(lax.rem(z + step + 16, 16))
            else:
                ref = of(lands if landing else piece, rows, first, second)
                name = first if axis == "first" else second
                there = dict(place)
                there[name] = lax.rem(place[name] + step + 4, 4)
                to = device(z, there["y"], there["x"], core)
            return pltpu.make_async_remote_copy(
                src_ref=ref, dst_ref=ref, send_sem=op_send.at[number], recv_sem=op_recv.at[number],
                device_id=to, device_id_type=ONTO)

        return around, copy

    def by_color(body):
        for color in (0, 1):
            @pl.when(core == color)
            def _():
                body(*spread(color))

    def spread_start(around, copy):
        for number in range(7):
            copy(number).start()

        @pl.loop(1, 16)
        def _(step):
            target = lax.rem(p + step, 16)
            around_copy(around, p, target, p).start()

    def around_copy(around, source_slot, to, source):
        ref = op.at[zl, source_slot // 4, lax.rem(source_slot, 4), pl.ds(around[0], around[1])]
        return plane_copy(4, ref, ref, to, source)

    def spread_on(around, copy):
        for number in range(7):
            copy(number, True).wait_recv()
        for number in range(*MARKS["start"]):
            copy(number).start()

        @pl.loop(1, 16)
        def _(step):
            other = lax.rem(p + step, 16)
            around_copy(around, other, other, other).wait_recv()

        for number in range(*MARKS["ring"]):
            copy(number).start()
        follow_on(EARLY[:4], copy)

    def follow_on(steps, copy):
        for number, (low, high) in steps:
            copy(number, True).wait_recv()
            for follow in range(low, high):
                copy(follow).start()

    def spread_rest(around, copy):
        follow_on(EARLY[4:] + LATE, copy)
        for number in range(len(PLAN)):
            if PLAN[number][1][0] == "core":
                copy(number, True).wait_recv()

    def spread_sent(around, copy):
        for number in range(len(PLAN)):
            copy(number).wait_send()

        @pl.loop(1, 16)
        def _(step):
            other = lax.rem(p + step, 16)
            around_copy(around, p, other, other).wait_send()

    def window(target):
        return pl.ds(pl.multiple_of((3 * (target // 2) + lax.rem(target, 2)) * 128, 128), 256)

    half = pl.ds(pl.multiple_of(lax.rem(p, 2) * 64, 64), 192)
    mine24 = pl.ds(pl.multiple_of(p * 24, 8), 24)

    def turn_rows(grid, zs):
        for k in range(3):
            rows = slice(128 * k, 128 * k + 128)
            turn[0:128, :] = grid[rows, 0:128].T
            turn[128:256, :] = grid[rows, 128:256].T
            columns = turn[half, :]
            for target in range(16):
                zs[target, 12 * k:12 * k + 12, :] = columns[12 * target:12 * target + 12]

    own_lane = lax.broadcasted_iota(jnp.int32, (36, 128), 0) == lax.broadcasted_iota(jnp.int32, (36, 128), 1)

    def encode(zs, codes, target):
        value = zs[target]
        top = jnp.maximum(jnp.max(jnp.abs(value), axis=1, keepdims=True), 1e-30)
        level = jnp.ceil(jnp.log2(top) * 128.0)
        scaled = jnp.round(value * (jnp.exp2(level * (-1.0 / 128.0)) * 32700.0))
        levels = jnp.sum(jnp.where(own_lane, level, 0.0), axis=0, keepdims=True)
        whole = jnp.concatenate([scaled, jnp.broadcast_to(levels, (4, 128))], axis=0)
        codes[target] = whole.astype(jnp.int32).astype(jnp.int16)

    def decode(kind, codes, zb):
        @pl.loop(0, 4)
        def _(step):
            ways = (2 * step - 8, 7 - 2 * step, 2 * step - 7, 6 - 2 * step)
            for one, way in enumerate(ways):
                source = lax.rem(z + 16 + way, 16)
                arriving = z_copy(kind, codes.at[source], codes.at[source], source, source)
                if one < 3:
                    arriving.wait_recv()
                else:
                    pl.when(step < 3)(arriving.wait_recv)
            for way in ways:
                source = lax.rem(z + 16 + way, 16)
                whole = codes[source].astype(jnp.int32).astype(F32)
                levels = jnp.broadcast_to(whole[36:37], (36, 128))
                level = jnp.sum(jnp.where(own_lane, levels, 0.0), axis=1, keepdims=True)
                zb[source] = whole[0:36] * (jnp.exp2(level * (1.0 / 128.0)) * (1.0 / 32700.0))

    def send_z(kind, zs, zb, target):
        @pl.when(target != z)
        def _():
            z_copy(kind, zs.at[target], zb.at[z], target, z).start()

        @pl.when(target == z)
        def _():
            zb[z] = zs[z]

    def send_all_z(kind, zs, codes, landing):
        @pl.loop(0, 4)
        def _(step):
            group = [lax.rem(z + 16 + way, 16) for way in
                     (2 * step - 8, 7 - 2 * step, 2 * step - 7, 6 - 2 * step)]
            for target in group:
                encode(zs, codes, target)
            for target in group:
                send_z(kind, codes, landing, target)

    def turn_columns(zb, rows_out):
        for k in range(3):
            turn[half, :] = jnp.concatenate([zb[source, 12 * k:12 * k + 12, :] for source in range(16)], axis=0)
            rows = slice(128 * k, 128 * k + 128)
            rows_out[rows, 0:128] = turn[0:128, :].T
            rows_out[rows, 128:256] = turn[128:256, :].T

    def send_rows(kind, rows_out, ib):
        @pl.loop(1, 16)
        def _(step):
            target = lax.rem(p + step, 16)
            plane_copy(kind, rows24(rows_out, target), ib.at[p], target, p).start()

        ib[p] = rows_out[mine24, :]

    low_lanes = lax.broadcasted_iota(jnp.int32, (24, 128), 1) < 64

    def merged(ib, m):
        even, odd = ib[2 * m], ib[2 * m + 1]
        return even[:, 0:128], jnp.where(low_lanes, even[:, 128:256], odd[:, 0:128]), odd[:, 128:256]

    def block(m, ii, f):
        row = ii * 1280 + f * 128
        parts, left = [], 128
        while left:
            place, offset = divmod(row, 240)
            take = min(left, 240 - offset)
            parts.append(op[m, place // 4, place % 4, offset:offset + take, :])
            row, left = row + take, left - take
        return parts[0] if len(parts) == 1 else jnp.concatenate(parts, axis=0)

    def outward(step):
        return jnp.where(lax.rem(step, 2) == 1, (step + 1) // 2, 8 - step // 2)

    def operate(first, emit, after=None, order=lambda step: step):
        @pl.loop(0, 8)
        def _(step):
            m = lax.rem(first + order(step), 8)
            for ii in range(3):
                vectors = jnp.concatenate([xb[cols_ref[f, 3 * m + ii]] for f in range(10)], axis=1)
                blocks = jnp.concatenate([block(m, ii, f) for f in range(10)], axis=1)
                both = lax.dot_general(vectors, blocks, (((1,), (1,)), ((), ())), preferred_element_type=F32)
                emit(m, ii, both[0:24] + both[24:48])
            if after is not None:
                after(m)

    def lanes(m, ii):
        return pl.ds(pl.multiple_of((3 * m + ii) * 128, 128), 128)

    by_color(spread_start)
    load_v.wait()

    @pl.loop(1, 16)
    def _(step):
        target = lax.rem(p + step, 16)
        plane_copy(0, v_ref.at[:, window(target)], grid_v.at[mine24, :], target, p).start()


    energy = shift_ref[0]
    eb[zh] = jnp.full((8, 128), energy, F32)
    turn[...] = jnp.zeros_like(turn)
    load_diag.wait()
    grid_v[pl.ds(pl.multiple_of(p * 24, 8), 24), :] = v_ref[
        :, pl.ds(pl.multiple_of((3 * (p // 2) + lax.rem(p, 2)) * 128, 128), 256)]

    @pl.loop(0, 24)
    def _(c):
        xb[c] = split(v_ref[:, pl.ds(pl.multiple_of(c * 128, 128), 128)])

    by_color(spread_on)
    pl.semaphore_wait(vouch, 2)
    energy_copy = pltpu.make_async_remote_copy(
        src_ref=eb.at[zh], dst_ref=eb.at[zh], send_sem=pair_send.at[2], recv_sem=pair_recv.at[2],
        device_id=at_z(lax.rem(z + 8, 16)), device_id_type=ONTO)
    energy_copy.start()
    wait_plane(0, lambda other: rows24(grid_v, other))
    turn_rows(grid_v, zs_v)
    send_all_z(0, zs_v, sent_v, got_v)
    by_color(spread_rest)

    def emit_t(m, ii, value):
        here = lanes(m, ii)
        tb[m, :, 128 * ii:128 * ii + 128] = value + (diag_ref[:, here] - energy) * v_ref[:, here]

    def after_t(m):
        for odd in (0, 1):
            target = 2 * m + odd
            part = tb.at[m, :, pl.ds(128 * odd, 256)]

            @pl.when(target != p)
            def _():
                plane_copy(1, part, grid_t.at[mine24, :], target, p).start()

            @pl.when(target == p)
            def _():
                grid_t[mine24, :] = tb[m, :, 128 * odd:128 * odd + 256]

    operate(lax.rem(p // 2 + 1, 8), emit_t, after_t)

    wait_plane(1, lambda other: rows24(grid_t, other))
    turn_rows(grid_t, zs_t)
    send_all_z(1, zs_t, sent_t, got_t)

    decode(0, got_v, zb_v)

    @pl.loop(0, 8)
    def _(m):
        for k in range(3):
            part = slice(12 * k, 12 * k + 12)
            both = jnp.concatenate([zb_v[m, part, :], zb_v[8 + m, part, :]], axis=0)
            vc[3 * m + k] = both
            xb[3 * m + k] = split(both)

    def emit_rv(m, ii, value):
        rv[3 * m + ii] = value

    operate(0, emit_rv)
    decode(1, got_t, zb_t)

    other_energy = pltpu.make_async_remote_copy(
        src_ref=eb.at[1 - zh], dst_ref=eb.at[1 - zh], send_sem=pair_send.at[2], recv_sem=pair_recv.at[2],
        device_id=at_z(lax.rem(z + 8, 16)), device_id_type=ONTO)
    other_energy.wait_recv()
    upper = lax.broadcasted_iota(jnp.int32, (24, 128), 0) < 12
    shifts = jnp.where(upper, jnp.broadcast_to(eb[0, 0:1, :], (24, 128)), jnp.broadcast_to(eb[1, 0:1, :], (24, 128)))

    def weights(to_core):
        straight = jnp.where(upper, rot_ref[to_core, core], rot_ref[2 + to_core, 2 + core])
        crossed = jnp.where(upper, rot_ref[to_core, 2 + core], rot_ref[2 + to_core, core])
        return straight, crossed

    here_straight, here_crossed = weights(core)
    there_straight, there_crossed = weights(1 - core)

    def swapped(value):
        return jnp.concatenate([value[12:24], value[0:12]], axis=0)

    def pair_copy(index, src, dst):
        return pltpu.make_async_remote_copy(
            src_ref=src, dst_ref=dst, send_sem=pair_send.at[index], recv_sem=pair_recv.at[index],
            device_id=pair, device_id_type=ONTO)

    @pl.loop(0, 8)
    def _(m):
        for k in range(3):
            c = 3 * m + k
            part = slice(12 * k, 12 * k + 12)
            t = jnp.concatenate([zb_t[m, part, :], zb_t[8 + m, part, :]], axis=0)
            first = 0.5 * (rv[c] + t)
            turned = swapped(first)
            rv[c] = first
            fm[c] = here_straight * first + here_crossed * turned
            fsib[c] = there_straight * first + there_crossed * turned

    pair_copy(0, fsib, fr).start()

    @pl.loop(0, 8)
    def _(m):
        for k in range(3):
            c = 3 * m + k
            rest = shifts * rv[c] + vc[c]
            rest_turned = swapped(rest)
            pm[c] = here_straight * rest + here_crossed * rest_turned
            psib[c] = there_straight * rest + there_crossed * rest_turned

    pair_copy(1, psib, pr).start()
    pair_copy(0, fsib, fr).wait_recv()

    @pl.loop(0, 8)
    def _(step):
        m = lax.rem(zl + outward(step), 8)
        for k in range(3):
            c = 3 * m + k
            value = fm[c] + fr[c]
            xb[c] = split(value)
            zs_f[m, 12 * k:12 * k + 12, :] = value[0:12]
            zs_f[8 + m, 12 * k:12 * k + 12, :] = value[12:24]
        encode(zs_f, sent_f, m)
        encode(zs_f, sent_f, m + 8)
        send_z(2, sent_f, got_f, m)
        send_z(2, sent_f, got_f, m + 8)

    pair_copy(1, psib, pr).wait_recv()

    def emit_g(m, ii, value):
        c = 3 * m + ii
        g = value - (pm[c] + pr[c])
        zs_g[m, 12 * ii:12 * ii + 12, :] = g[0:12]
        zs_g[8 + m, 12 * ii:12 * ii + 12, :] = g[12:24]

    def after_g(m):
        encode(zs_g, sent_g, m)
        encode(zs_g, sent_g, m + 8)
        send_z(3, sent_g, got_g, m)
        send_z(3, sent_g, got_g, m + 8)

    operate(zl, emit_g, after_g, outward)

    decode(2, got_f, zb_f)
    turn_columns(zb_f, wf)
    send_rows(2, wf, ib_f)
    decode(3, got_g, zb_g)
    turn_columns(zb_g, wg)
    send_rows(3, wg, ib_g)
    wait_plane(2, lambda other: ib_f.at[other])

    @pl.loop(0, 8)
    def _(m):
        for ii, tile in enumerate(merged(ib_f, m)):
            hf[m, :, 128 * ii:128 * ii + 128] = tile
            xb[3 * m + ii] = split(tile)

    def emit_out(m, ii, value):
        here = lanes(m, ii)
        out_ref[:, here] = value + diag_ref[:, here] * hf[m, :, 128 * ii:128 * ii + 128]

    operate(0, emit_out)
    wait_plane(3, lambda other: ib_g.at[other])

    @pl.loop(0, 8)
    def _(m):
        for ii, tile in enumerate(merged(ib_g, m)):
            here = lanes(m, ii)
            out_ref[:, here] = out_ref[:, here] + tile

    by_color(spread_sent)
    energy_copy.wait_send()
    pair_copy(0, fsib, fr).wait_send()
    pair_copy(1, psib, pr).wait_send()
    sent_plane(0, lambda other: rows24(grid_v, other))
    sent_plane(1, lambda other: rows24(grid_t, other))
    sent_plane(2, lambda other: ib_f.at[other])
    sent_plane(3, lambda other: ib_g.at[other])
    for kind, ref in enumerate((sent_v, sent_t, sent_f, sent_g)):
        sent_z(kind, ref)


def shards(coeffs, diagonal, shift, rotation, string_blocks, block_cols):
    vmem = pl.BlockSpec(memory_space=pltpu.VMEM)
    smem = pl.BlockSpec(memory_space=pltpu.SMEM)
    hbm = pl.BlockSpec(memory_space=pltpu.HBM)
    rows = pltpu.VMEM((24, 3072), F32)
    grid = pltpu.VMEM((384, 256), F32)
    packed = pltpu.VMEM((16, 36, 128), F32)
    coded = pltpu.VMEM((16, 40, 128), jnp.int16)
    chunks = pltpu.VMEM((24, 24, 128), F32)
    windows = pltpu.VMEM((16, 24, 256), F32)
    wide = pltpu.VMEM((8, 24, 384), F32)
    dma = pltpu.SemaphoreType.DMA
    result = pl.pallas_call(
        kernel,
        out_shape=jax.ShapeDtypeStruct((24, 3072), F32),
        in_specs=[hbm, hbm, smem, smem, hbm, smem],
        out_specs=vmem,
        scratch_shapes=[
            rows, rows, pltpu.VMEM((8, 4, 4, 240, 128), BF16),
            grid, grid, pltpu.VMEM((256, 128), F32),
            packed, packed, packed, packed, packed, packed, packed, packed,
            coded, coded, coded, coded, coded, coded, coded, coded,
            pltpu.VMEM((24, 48, 128), BF16),
            chunks, chunks, wide,
            chunks, chunks, chunks, chunks, chunks, chunks,
            grid, grid, windows, windows, wide,
            pltpu.VMEM((2, 8, 128), F32),
            dma((len(PLAN),)), dma((len(PLAN),)), dma((3,)),
            dma((5, 16)), dma((5, 16)), dma((4, 16)), dma((4, 16)), dma((3,)), dma((3,)),
            pltpu.SemaphoreType.REGULAR,
        ],
        compiler_params=pltpu.CompilerParams(
            collective_id=0, has_side_effects=True, vmem_limit_bytes=50331648),
        name="filter",
    )(*(pltpu.with_memory_space_constraint(a, pltpu.HBM) for a in (coeffs, diagonal)), shift, rotation,
      pltpu.with_memory_space_constraint(string_blocks, pltpu.HBM), block_cols.T)
    return result[None]


def solution(mesh):
    split_mesh = Mesh(mesh.devices.reshape(2, 2, 8, 4, 4), ROOT + COL)
    return jax.shard_map(
        shards,
        mesh=split_mesh,
        in_specs=(P(ROOT, COL, None), P(COL, None), P(ROOT), P(), P(COL, None), P()),
        out_specs=P(ROOT, COL, None),
        check_vma=False,
    )
```

```python
import jax
import jax.numpy as jnp
from jax import lax
from jax.experimental import pallas as pl
from jax.experimental.pallas import tpu as pltpu
from jax.sharding import Mesh
from jax.sharding import PartitionSpec as P

ROOT = ("zh", "core")
COL = ("zl", "y", "x")
CUT = 128
PARTS = (((0, 96), (96, 32)), ((CUT, 80), (CUT + 80, 32)))
F32, BF16 = jnp.float32, jnp.bfloat16
ONTO = pl.DeviceIdType.MESH

E, H, Q = (0, 8), ((0, 4), (4, 4)), ((0, 2), (2, 2), (4, 2), (6, 2))
Z_STEPS = (1, -1, 2, -2, 3, -3, 4)


def spread_plan():
    plan = [("z", ("z", d), None) for d in Z_STEPS]

    def both(zs, a):
        plan.append(((zs, a, 0), ("second", 1), (zs, a, -1)))
        plan.append(((zs, a, 0), ("second", -1), (zs, a, 1)))

    def sibling(zs, a, b):
        plan.append(((zs, a, b), ("core", 1), "sibling"))

    plan.append(((E, 0, 0), ("first", 1), (E, -1, 0)))
    plan.append(((E, 0, 0), ("first", -1), (E, 1, 0)))
    both(E, 0)
    sibling(E, 0, 0)
    marks = {"start": (7, 12)}
    steps = []
    n = len(plan)
    plan.append(((H[0], -1, 0), ("first", 1), (H[0], -2, 0)))
    both(E, -1)
    sibling(E, -1, 0)
    steps.append((7, (n, len(plan))))
    far_low = n
    n = len(plan)
    plan.append(((H[1], 1, 0), ("first", -1), (H[1], 2, 0)))
    both(E, 1)
    sibling(E, 1, 0)
    steps.append((8, (n, len(plan))))
    far_high = n
    n = len(plan)
    both(H[0], 2)
    sibling(H[0], 2, 0)
    steps.append((far_low, (n, len(plan))))
    n = len(plan)
    both(H[1], 2)
    sibling(H[1], 2, 0)
    steps.append((far_high, (n, len(plan))))
    sets = [(0, E, H[0], H[1], 9), (-1, E, H[0], H[1], 13), (1, E, H[0], H[1], 17),
            (2, H[0], Q[0], Q[1], 20), (2, H[1], Q[2], Q[3], 23)]
    last = []
    for a, zs, low, high, number in sets:
        n = len(plan)
        plan.append(((low, a, -1), ("second", 1), (low, a, -2)))
        sibling(zs, a, -1)
        steps.append((number, (n, len(plan))))
        last.append((n, low, a))
        n = len(plan)
        plan.append(((high, a, 1), ("second", -1), (high, a, 2)))
        sibling(zs, a, 1)
        steps.append((number + 1, (n, len(plan))))
        last.append((n, high, a))
    lasts = []
    for number, zs, a in last:
        n = len(plan)
        sibling(zs, a, 2)
        lasts.append((number, (n, len(plan))))

    def ring(part, half, way):
        plan.append((("ring", part, half), ("z", way), ("ring", part - way, half)))
        return len(plan) - 1

    def ring_sibling(part, half=None):
        plan.append((("ring", part, half), ("core", 1), "sibling"))

    n = len(plan)
    up, down = ring(0, None, 1), ring(0, None, -1)
    ring_sibling(0)
    marks["ring"] = (n, len(plan))
    rings = []
    for hop in (1, 2, 3):
        n = len(plan)
        next_up = ring(-hop, 0 if hop == 3 else None, 1)
        ring_sibling(-hop)
        rings.append((up, (n, len(plan))))
        n = len(plan)
        next_down = ring(hop, 1 if hop == 3 else None, -1)
        ring_sibling(hop)
        rings.append((down, (n, len(plan))))
        up, down = next_up, next_down
    for number, part, half in ((up, -4, 0), (down, 4, 1)):
        n = len(plan)
        ring_sibling(part, half)
        rings.append((number, (n, len(plan))))
    early = steps[0:2] + rings[0:2] + steps[2:8] + rings[2:4] + steps[8:12] + rings[4:6]
    late = steps[12:] + lasts + rings[6:8]
    return plan, marks, early, late


PLAN, MARKS, EARLY, LATE = spread_plan()


def device(z, y, x, core):
    return {"zh": z // 8, "core": core, "zl": lax.rem(z, 8), "y": y, "x": x}


def split(value):
    high = value.astype(BF16).astype(F32)
    return jnp.concatenate([high, value - high], axis=0).astype(BF16)


def kernel(v_any, diag_any, shift_ref, rot_ref, mine_ref, cols_ref, out_ref,
           v_ref, diag_ref, op, grid_v, grid_t, turn, zs_v, zs_t, zs_f, zs_g, zb_v, zb_t, zb_f, zb_g,
           sent_v, sent_t, sent_f, sent_g, got_v, got_t, got_f, got_g,
           xb, vc, rv, tb, fm, fsib, pm, psib, fr, pr, wf, wg, ib_f, ib_g, hf, eb,
           op_send, op_recv, local, plane_send, plane_recv, z_send, z_recv, pair_send, pair_recv, vouch):
    zh, core, zl = lax.axis_index("zh"), lax.axis_index("core"), lax.axis_index("zl")
    y, x = lax.axis_index("y"), lax.axis_index("x")
    z = zh * 8 + zl
    p = y * 4 + x

    def at_z(other):
        return device(other, y, x, core)

    def at_p(other):
        return {"zh": zh, "core": core, "zl": zl, "y": other // 4, "x": lax.rem(other, 4)}

    pair = {"zh": zh, "core": 1 - core, "zl": zl, "y": y, "x": x}

    barrier = pltpu.get_barrier_semaphore()

    @pl.loop(1, 16)
    def _(step):
        pl.semaphore_signal(barrier, inc=1, device_id=at_p(lax.rem(p + step, 16)), device_id_type=ONTO)

    for step in (4, -4, 3, -3, 2, -2, 1, -1):
        pl.semaphore_signal(barrier, inc=1, device_id=at_z(lax.rem(z + step + 16, 16)), device_id_type=ONTO)

    pl.semaphore_signal(barrier, inc=1, device_id=pair, device_id_type=ONTO)
    load_v = pltpu.make_async_copy(v_any.at[0], v_ref, local.at[0])
    load_diag = pltpu.make_async_copy(diag_any, diag_ref, local.at[1])
    @pl.when(core == 0)
    def _():
        part = pl.ds(0, CUT)
        load = pltpu.make_async_copy(mine_ref.at[part], op.at[zl, y, x, part], local.at[2])
        load.start()
        load_v.start()
        load_diag.start()
        load.wait()

    @pl.when(core == 1)
    def _():
        part = pl.ds(CUT, 240 - CUT)
        load = pltpu.make_async_copy(mine_ref.at[part], op.at[zl, y, x, part], local.at[2])
        load.start()
        load_v.start()
        load_diag.start()
        load.wait()

    pl.semaphore_wait(barrier, 24)
    for step in (4, -4):
        pl.semaphore_signal(vouch, inc=1, device_id=at_z(lax.rem(z + step + 16, 16)), device_id_type=ONTO)

    def plane_copy(kind, src, dst, to, source):
        return pltpu.make_async_remote_copy(
            src_ref=src, dst_ref=dst, send_sem=plane_send.at[kind, to], recv_sem=plane_recv.at[kind, source],
            device_id=at_p(to), device_id_type=ONTO)

    def z_copy(kind, src, dst, to, source):
        return pltpu.make_async_remote_copy(
            src_ref=src, dst_ref=dst, send_sem=z_send.at[kind, to], recv_sem=z_recv.at[kind, source],
            device_id=at_z(to), device_id_type=ONTO)

    def rows24(ref, index):
        return ref.at[pl.ds(pl.multiple_of(index * 24, 8), 24), :]

    def wait_plane(kind, slot):
        @pl.loop(1, 16)
        def _(step):
            other = lax.rem(p + step, 16)
            plane_copy(kind, slot(other), slot(other), other, other).wait_recv()

    def sent_plane(kind, slot):
        @pl.loop(1, 16)
        def _(step):
            other = lax.rem(p + step, 16)
            plane_copy(kind, slot(other), slot(other), other, other).wait_send()

    def sent_z(kind, ref):
        @pl.loop(1, 16)
        def _(step):
            other = lax.rem(z + step, 16)
            z_copy(kind, ref.at[other], ref.at[other], other, other).wait_send()

    def spread(color):
        rows, around = PARTS[color]
        others, others_around = PARTS[1 - color]
        place = {"y": y, "x": x}

        def of(piece, part, first, second):
            zs, a, b = piece
            if zs == "ring":
                which = pl.ds(0, 4) if b is None else pl.ds(2 * b, 2)
                return op.at[lax.rem(zl + a + 8, 8), which, :, pl.ds(part[0], part[1])]
            index = {first: lax.rem(place[first] + a + 4, 4), second: lax.rem(place[second] + b + 4, 4)}
            return op.at[pl.ds(zs[0], zs[1]), index["y"], index["x"], pl.ds(part[0], part[1])]

        first, second = ("y", "x") if color == 0 else ("x", "y")

        def copy(number, landing=False):
            piece, (axis, step), lands = PLAN[number]
            if piece == "z":
                source = lax.rem(zl - step + 8, 8) if landing else zl
                ref = op.at[source, y, x, pl.ds(rows[0], rows[1])]
                to = at_z(lax.rem(z + step + 16, 16))
            elif axis == "core":
                going = around if piece[0] == "ring" else rows
                coming = others_around if piece[0] == "ring" else others
                ref = of(piece, coming, second, first) if landing else of(piece, going, first, second)
                to = pair
            elif axis == "z":
                ref = of(lands if landing else piece, around, first, second)
                to = at_z(lax.rem(z + step + 16, 16))
            else:
                ref = of(lands if landing else piece, rows, first, second)
                name = first if axis == "first" else second
                there = dict(place)
                there[name] = lax.rem(place[name] + step + 4, 4)
                to = device(z, there["y"], there["x"], core)
            return pltpu.make_async_remote_copy(
                src_ref=ref, dst_ref=ref, send_sem=op_send.at[number], recv_sem=op_recv.at[number],
                device_id=to, device_id_type=ONTO)

        return around, copy

    def by_color(body):
        for color in (0, 1):
            @pl.when(core == color)
            def _():
                body(*spread(color))

    def spread_start(around, copy):
        for number in range(7):
            copy(number).start()

        @pl.loop(1, 16)
        def _(step):
            target = lax.rem(p + step, 16)
            around_copy(around, p, target, p).start()

    def around_copy(around, source_slot, to, source):
        ref = op.at[zl, source_slot // 4, lax.rem(source_slot, 4), pl.ds(around[0], around[1])]
        return plane_copy(4, ref, ref, to, source)

    def spread_on(around, copy):
        for number in range(7):
            copy(number, True).wait_recv()
        for number in range(*MARKS["start"]):
            copy(number).start()

        @pl.loop(1, 16)
        def _(step):
            other = lax.rem(p + step, 16)
            around_copy(around, other, other, other).wait_recv()

        for number in range(*MARKS["ring"]):
            copy(number).start()
        follow_on(EARLY[:4], copy)

    def follow_on(steps, copy):
        for number, (low, high) in steps:
            copy(number, True).wait_recv()
            for follow in range(low, high):
                copy(follow).start()

    def spread_rest(around, copy):
        follow_on(EARLY[4:] + LATE, copy)
        for number in range(len(PLAN)):
            if PLAN[number][1][0] == "core":
                copy(number, True).wait_recv()

    def spread_sent(around, copy):
        for number in range(len(PLAN)):
            copy(number).wait_send()

        @pl.loop(1, 16)
        def _(step):
            other = lax.rem(p + step, 16)
            around_copy(around, p, other, other).wait_send()

    def window(target):
        return pl.ds(pl.multiple_of((3 * (target // 2) + lax.rem(target, 2)) * 128, 128), 256)

    half = pl.ds(pl.multiple_of(lax.rem(p, 2) * 64, 64), 192)
    mine24 = pl.ds(pl.multiple_of(p * 24, 8), 24)

    def turn_rows(grid, zs):
        for k in range(3):
            rows = slice(128 * k, 128 * k + 128)
            turn[0:128, :] = grid[rows, 0:128].T
            turn[128:256, :] = grid[rows, 128:256].T
            columns = turn[half, :]
            for target in range(16):
                zs[target, 12 * k:12 * k + 12, :] = columns[12 * target:12 * target + 12]

    own_lane = lax.broadcasted_iota(jnp.int32, (36, 128), 0) == lax.broadcasted_iota(jnp.int32, (36, 128), 1)

    def encode(zs, codes, target):
        value = zs[target]
        top = jnp.maximum(jnp.max(jnp.abs(value), axis=1, keepdims=True), 1e-30)
        level = jnp.ceil(jnp.log2(top) * 128.0)
        scaled = jnp.round(value * (jnp.exp2(level * (-1.0 / 128.0)) * 32700.0))
        levels = jnp.sum(jnp.where(own_lane, level, 0.0), axis=0, keepdims=True)
        whole = jnp.concatenate([scaled, jnp.broadcast_to(levels, (4, 128))], axis=0)
        codes[target] = whole.astype(jnp.int32).astype(jnp.int16)

    def decode(kind, codes, zb):
        @pl.loop(0, 4)
        def _(step):
            ways = (2 * step - 8, 7 - 2 * step, 2 * step - 7, 6 - 2 * step)
            for one, way in enumerate(ways):
                source = lax.rem(z + 16 + way, 16)
                arriving = z_copy(kind, codes.at[source], codes.at[source], source, source)
                if one < 3:
                    arriving.wait_recv()
                else:
                    pl.when(step < 3)(arriving.wait_recv)
            for way in ways:
                source = lax.rem(z + 16 + way, 16)
                whole = codes[source].astype(jnp.int32).astype(F32)
                levels = jnp.broadcast_to(whole[36:37], (36, 128))
                level = jnp.sum(jnp.where(own_lane, levels, 0.0), axis=1, keepdims=True)
                zb[source] = whole[0:36] * (jnp.exp2(level * (1.0 / 128.0)) * (1.0 / 32700.0))

    def send_z(kind, zs, zb, target):
        @pl.when(target != z)
        def _():
            z_copy(kind, zs.at[target], zb.at[z], target, z).start()

        @pl.when(target == z)
        def _():
            zb[z] = zs[z]

    def send_all_z(kind, zs, codes, landing):
        @pl.loop(0, 4)
        def _(step):
            group = [lax.rem(z + 16 + way, 16) for way in
                     (2 * step - 8, 7 - 2 * step, 2 * step - 7, 6 - 2 * step)]
            for target in group:
                encode(zs, codes, target)
            for target in group:
                send_z(kind, codes, landing, target)

    def turn_columns(zb, rows_out):
        for k in range(3):
            turn[half, :] = jnp.concatenate([zb[source, 12 * k:12 * k + 12, :] for source in range(16)], axis=0)
            rows = slice(128 * k, 128 * k + 128)
            rows_out[rows, 0:128] = turn[0:128, :].T
            rows_out[rows, 128:256] = turn[128:256, :].T

    def send_rows(kind, rows_out, ib):
        @pl.loop(1, 16)
        def _(step):
            target = lax.rem(p + step, 16)
            plane_copy(kind, rows24(rows_out, target), ib.at[p], target, p).start()

        ib[p] = rows_out[mine24, :]

    low_lanes = lax.broadcasted_iota(jnp.int32, (24, 128), 1) < 64

    def merged(ib, m):
        even, odd = ib[2 * m], ib[2 * m + 1]
        return even[:, 0:128], jnp.where(low_lanes, even[:, 128:256], odd[:, 0:128]), odd[:, 128:256]

    def block(m, ii, f):
        row = ii * 1280 + f * 128
        parts, left = [], 128
        while left:
            place, offset = divmod(row, 240)
            take = min(left, 240 - offset)
            parts.append(op[m, place // 4, place % 4, offset:offset + take, :])
            row, left = row + take, left - take
        return parts[0] if len(parts) == 1 else jnp.concatenate(parts, axis=0)

    def outward(step):
        return jnp.where(lax.rem(step, 2) == 1, (step + 1) // 2, 8 - step // 2)

    def operate(first, emit, after=None, order=lambda step: step):
        @pl.loop(0, 8)
        def _(step):
            m = lax.rem(first + order(step), 8)
            for ii in range(3):
                vectors = jnp.concatenate([xb[cols_ref[f, 3 * m + ii]] for f in range(10)], axis=1)
                blocks = jnp.concatenate([block(m, ii, f) for f in range(10)], axis=1)
                both = lax.dot_general(vectors, blocks, (((1,), (1,)), ((), ())), preferred_element_type=F32)
                emit(m, ii, both[0:24] + both[24:48])
            if after is not None:
                after(m)

    def lanes(m, ii):
        return pl.ds(pl.multiple_of((3 * m + ii) * 128, 128), 128)

    by_color(spread_start)
    load_v.wait()

    @pl.loop(1, 16)
    def _(step):
        target = lax.rem(p + step, 16)
        plane_copy(0, v_ref.at[:, window(target)], grid_v.at[mine24, :], target, p).start()


    energy = shift_ref[0]
    eb[zh] = jnp.full((8, 128), energy, F32)
    turn[...] = jnp.zeros_like(turn)
    load_diag.wait()
    grid_v[pl.ds(pl.multiple_of(p * 24, 8), 24), :] = v_ref[
        :, pl.ds(pl.multiple_of((3 * (p // 2) + lax.rem(p, 2)) * 128, 128), 256)]

    @pl.loop(0, 24)
    def _(c):
        xb[c] = split(v_ref[:, pl.ds(pl.multiple_of(c * 128, 128), 128)])

    by_color(spread_on)
    pl.semaphore_wait(vouch, 2)
    energy_copy = pltpu.make_async_remote_copy(
        src_ref=eb.at[zh], dst_ref=eb.at[zh], send_sem=pair_send.at[2], recv_sem=pair_recv.at[2],
        device_id=at_z(lax.rem(z + 8, 16)), device_id_type=ONTO)
    energy_copy.start()
    wait_plane(0, lambda other: rows24(grid_v, other))
    turn_rows(grid_v, zs_v)
    send_all_z(0, zs_v, sent_v, got_v)
    by_color(spread_rest)

    def emit_t(m, ii, value):
        here = lanes(m, ii)
        tb[m, :, 128 * ii:128 * ii + 128] = value + (diag_ref[:, here] - energy) * v_ref[:, here]

    def after_t(m):
        for odd in (0, 1):
            target = 2 * m + odd
            part = tb.at[m, :, pl.ds(128 * odd, 256)]

            @pl.when(target != p)
            def _():
                plane_copy(1, part, grid_t.at[mine24, :], target, p).start()

            @pl.when(target == p)
            def _():
                grid_t[mine24, :] = tb[m, :, 128 * odd:128 * odd + 256]

    operate(lax.rem(p // 2 + 1, 8), emit_t, after_t)

    wait_plane(1, lambda other: rows24(grid_t, other))
    turn_rows(grid_t, zs_t)
    send_all_z(1, zs_t, sent_t, got_t)

    decode(0, got_v, zb_v)

    @pl.loop(0, 8)
    def _(m):
        for k in range(3):
            part = slice(12 * k, 12 * k + 12)
            both = jnp.concatenate([zb_v[m, part, :], zb_v[8 + m, part, :]], axis=0)
            vc[3 * m + k] = both
            xb[3 * m + k] = split(both)

    def emit_rv(m, ii, value):
        rv[3 * m + ii] = value

    operate(0, emit_rv)
    decode(1, got_t, zb_t)

    other_energy = pltpu.make_async_remote_copy(
        src_ref=eb.at[1 - zh], dst_ref=eb.at[1 - zh], send_sem=pair_send.at[2], recv_sem=pair_recv.at[2],
        device_id=at_z(lax.rem(z + 8, 16)), device_id_type=ONTO)
    other_energy.wait_recv()
    upper = lax.broadcasted_iota(jnp.int32, (24, 128), 0) < 12
    shifts = jnp.where(upper, jnp.broadcast_to(eb[0, 0:1, :], (24, 128)), jnp.broadcast_to(eb[1, 0:1, :], (24, 128)))

    def weights(to_core):
        straight = jnp.where(upper, rot_ref[to_core, core], rot_ref[2 + to_core, 2 + core])
        crossed = jnp.where(upper, rot_ref[to_core, 2 + core], rot_ref[2 + to_core, core])
        return straight, crossed

    here_straight, here_crossed = weights(core)
    there_straight, there_crossed = weights(1 - core)

    def swapped(value):
        return jnp.concatenate([value[12:24], value[0:12]], axis=0)

    def pair_copy(index, src, dst):
        return pltpu.make_async_remote_copy(
            src_ref=src, dst_ref=dst, send_sem=pair_send.at[index], recv_sem=pair_recv.at[index],
            device_id=pair, device_id_type=ONTO)

    @pl.loop(0, 8)
    def _(m):
        for k in range(3):
            c = 3 * m + k
            part = slice(12 * k, 12 * k + 12)
            t = jnp.concatenate([zb_t[m, part, :], zb_t[8 + m, part, :]], axis=0)
            first = 0.5 * (rv[c] + t)
            turned = swapped(first)
            rv[c] = first
            fm[c] = here_straight * first + here_crossed * turned
            fsib[c] = there_straight * first + there_crossed * turned

    pair_copy(0, fsib, fr).start()

    @pl.loop(0, 8)
    def _(m):
        for k in range(3):
            c = 3 * m + k
            rest = shifts * rv[c] + vc[c]
            rest_turned = swapped(rest)
            pm[c] = here_straight * rest + here_crossed * rest_turned
            psib[c] = there_straight * rest + there_crossed * rest_turned

    pair_copy(1, psib, pr).start()
    pair_copy(0, fsib, fr).wait_recv()

    @pl.loop(0, 8)
    def _(step):
        m = lax.rem(zl + outward(step), 8)
        for k in range(3):
            c = 3 * m + k
            value = fm[c] + fr[c]
            xb[c] = split(value)
            zs_f[m, 12 * k:12 * k + 12, :] = value[0:12]
            zs_f[8 + m, 12 * k:12 * k + 12, :] = value[12:24]
        encode(zs_f, sent_f, m)
        encode(zs_f, sent_f, m + 8)
        send_z(2, sent_f, got_f, m)
        send_z(2, sent_f, got_f, m + 8)

    pair_copy(1, psib, pr).wait_recv()

    def emit_g(m, ii, value):
        c = 3 * m + ii
        g = value - (pm[c] + pr[c])
        zs_g[m, 12 * ii:12 * ii + 12, :] = g[0:12]
        zs_g[8 + m, 12 * ii:12 * ii + 12, :] = g[12:24]

    def after_g(m):
        encode(zs_g, sent_g, m)
        encode(zs_g, sent_g, m + 8)
        send_z(3, sent_g, got_g, m)
        send_z(3, sent_g, got_g, m + 8)

    operate(zl, emit_g, after_g, outward)

    decode(2, got_f, zb_f)
    turn_columns(zb_f, wf)
    send_rows(2, wf, ib_f)
    decode(3, got_g, zb_g)
    turn_columns(zb_g, wg)
    send_rows(3, wg, ib_g)
    wait_plane(2, lambda other: ib_f.at[other])

    @pl.loop(0, 8)
    def _(m):
        for ii, tile in enumerate(merged(ib_f, m)):
            hf[m, :, 128 * ii:128 * ii + 128] = tile
            xb[3 * m + ii] = split(tile)

    def emit_out(m, ii, value):
        here = lanes(m, ii)
        out_ref[:, here] = value + diag_ref[:, here] * hf[m, :, 128 * ii:128 * ii + 128]

    operate(0, emit_out)
    wait_plane(3, lambda other: ib_g.at[other])

    @pl.loop(0, 8)
    def _(m):
        for ii, tile in enumerate(merged(ib_g, m)):
            here = lanes(m, ii)
            out_ref[:, here] = out_ref[:, here] + tile

    by_color(spread_sent)
    energy_copy.wait_send()
    pair_copy(0, fsib, fr).wait_send()
    pair_copy(1, psib, pr).wait_send()
    sent_plane(0, lambda other: rows24(grid_v, other))
    sent_plane(1, lambda other: rows24(grid_t, other))
    sent_plane(2, lambda other: ib_f.at[other])
    sent_plane(3, lambda other: ib_g.at[other])
    for kind, ref in enumerate((sent_v, sent_t, sent_f, sent_g)):
        sent_z(kind, ref)


def kept(value):
    return pltpu.with_memory_space_constraint(value, pltpu.HBM)


def shards(coeffs, diagonal, shift, rotation, string_blocks, block_cols):
    vmem = pl.BlockSpec(memory_space=pltpu.VMEM)
    smem = pl.BlockSpec(memory_space=pltpu.SMEM)
    hbm = pl.BlockSpec(memory_space=pltpu.HBM)
    rows = pltpu.VMEM((24, 3072), F32)
    grid = pltpu.VMEM((384, 256), F32)
    packed = pltpu.VMEM((16, 36, 128), F32)
    coded = pltpu.VMEM((16, 40, 128), jnp.int16)
    chunks = pltpu.VMEM((24, 24, 128), F32)
    windows = pltpu.VMEM((16, 24, 256), F32)
    wide = pltpu.VMEM((8, 24, 384), F32)
    dma = pltpu.SemaphoreType.DMA
    result = pl.pallas_call(
        kernel,
        out_shape=jax.ShapeDtypeStruct((24, 3072), F32),
        in_specs=[hbm, hbm, smem, smem, hbm, smem],
        out_specs=vmem,
        scratch_shapes=[
            rows, rows, pltpu.VMEM((8, 4, 4, 240, 128), BF16),
            grid, grid, pltpu.VMEM((256, 128), F32),
            packed, packed, packed, packed, packed, packed, packed, packed,
            coded, coded, coded, coded, coded, coded, coded, coded,
            pltpu.VMEM((24, 48, 128), BF16),
            chunks, chunks, wide,
            chunks, chunks, chunks, chunks, chunks, chunks,
            grid, grid, windows, windows, wide,
            pltpu.VMEM((2, 8, 128), F32),
            dma((len(PLAN),)), dma((len(PLAN),)), dma((3,)),
            dma((5, 16)), dma((5, 16)), dma((4, 16)), dma((4, 16)), dma((3,)), dma((3,)),
            pltpu.SemaphoreType.REGULAR,
        ],
        compiler_params=pltpu.CompilerParams(
            collective_id=0, has_side_effects=True, vmem_limit_bytes=50331648),
        name="filter",
    )(kept(coeffs), kept(diagonal), shift, kept(rotation), kept(string_blocks), kept(block_cols.T))
    return result[None]


def solution(mesh):
    split_mesh = Mesh(mesh.devices.reshape(2, 2, 8, 4, 4), ROOT + COL)
    return jax.shard_map(
        shards,
        mesh=split_mesh,
        in_specs=(P(ROOT, COL, None), P(COL, None), P(ROOT), P(), P(COL, None), P()),
        out_specs=P(ROOT, COL, None),
        check_vma=False,
    )
```
